32 devices in a mesh: pair: 8 (over z, y), chan: 4 (over x, core).
Axes of the slice: x: 2, y: 2, z: 4, core: 2. Of those that a mesh axis runs over, the one named last changes fastest.
Arguments:
- jones_init: float32 [512, 4, 128], P('pair', 'chan'), may hold values from -2 to 2
- dual_init: float32 [512, 4, 128], P('pair', 'chan'), may hold values from -1.2 to 1.2
- penalty: float32 [16], replicated, may hold values from 0.5 to 5
- sky_flux: float32 [4, 4, 16], P('chan'), may hold values from -0.1 to 0.5, as said below
- visibility: bfloat16 [8, 4, 8, 2, 128, 128], P('pair', 'chan'), may hold values from -4 to 4
- phases: float32 [8, 8, 2, 1024], P('pair'), may hold values from -3.1416 to 3.1416, as said below
- pair_ids: int32 [8], P('pair'), may hold values from 0 to 35, as said below
- counts: int32 [8], P('pair'), may hold values from 2 to 8, as said below
- slot_flags: int32 [8, 8], P('pair'), may hold values 0 or 1
Outputs:
- jones_final: float32 [512, 4, 128], P('pair', 'chan')
- duals_final: float32 [512, 4, 128], P('pair', 'chan')
- consensus: float32 [512, 3, 128], P('pair')
The draws below stay inside these ranges and needn't reach their ends.
Inputs may be any that keep to these rules, and one draw needn't show every extreme that they name: `sky_flux`: [f, 0, k] and [f, 1, k] are the two polarized fluxes, [f, 2, k] and [f, 3, k] the real and imaginary cross terms. `phases`: [t, s, 0, k * 64 + p] is the phase of direction k at row station p in slot s, [t, s, 1, ...] that at column station p, before scaling by frequency. `pair_ids`: block pair of each tile, numbered row by row over blocks a <= b of 8. A tile keeps slots 0 to counts - 1; tiles whose column block lies 8 // 2 or more blocks after their row block keep all 8.
All inputs are finite; a program needn't handle non-finite values. No bound on the sum of `slot_flags` on one device may be relied on, other than what follows from the above.
Results may differ from the reference program's by a relative error of at most 0.00076.
Values sent between devices are 32-bit elements; how exact they have to be, the bound alone decides.
A program may use at most 64 MiB of HBM per device.

```python
import math
import jax
import jax.numpy as jnp
import numpy as np
from jax import lax

STATIONS = 512
DIRS = 16
BLOCK = 64
JW = 128
NPAIRS = 36
CHANNELS = 4
TILES = 8
TIME = 8
NPOLY = 3
ITERS = 2
GSTEPS = 1


def table_pairs(block_count):
    row_list = []
    col_list = []
    for row_block in range(block_count):
        for col_block in range(row_block, block_count):
            row_list.append(row_block)
            col_list.append(col_block)
    return (np.array(row_list, np.int32), np.array(col_list, np.int32))


def pair_draw(key):
    picks = jax.random.randint(jax.random.fold_in(key, 11), (TILES,), 0, NPAIRS)
    where_top = jax.random.randint(jax.random.fold_in(key, 12), (), 0, TILES)
    return jnp.where(jnp.arange(TILES) == where_top, NPAIRS - 1, picks).astype(jnp.int32)


def draw_pair_ids(key, part):
    return pair_draw(key)


def draw_counts(key, part):
    pair_list = pair_draw(key)
    row_table, col_table = table_pairs(STATIONS // BLOCK)
    row_of = jnp.asarray(row_table)[pair_list]
    col_of = jnp.asarray(col_table)[pair_list]
    short_kept = jax.random.randint(jax.random.fold_in(key, 13), (TILES,), 2, TIME // 2 + 1)
    kept_slots = jnp.where(col_of - row_of >= STATIONS // BLOCK // 2, TIME, short_kept)
    full_at = jax.random.randint(jax.random.fold_in(key, 14), (), 0, TILES)
    return jnp.where(jnp.arange(TILES) == full_at, TIME, kept_slots).astype(jnp.int32)


def phase_draw(key):
    return jax.random.uniform(jax.random.fold_in(key, 21), (TILES, TIME, 2, DIRS * BLOCK), jnp.float32, -math.pi, math.pi)


def draw_phases(key, part):
    return phase_draw(key)


def sky_draw(key):
    freq_ratio = 1.0 + jnp.arange(CHANNELS, dtype=jnp.float32) / CHANNELS
    log_flux = jax.random.uniform(jax.random.fold_in(key, 15), (2, DIRS), jnp.float32, math.log(0.05), math.log(0.5))
    base_flux = jnp.exp(log_flux)
    base_flux = 0.5 * base_flux / jnp.max(base_flux)
    spectral = jax.random.uniform(jax.random.fold_in(key, 16), (1, 2, DIRS), jnp.float32, -1.0, -0.4)
    flux_all = base_flux[None] * freq_ratio[:, None, None] ** spectral
    cross_all = jnp.clip(0.05 * jax.random.normal(jax.random.fold_in(key, 17), (CHANNELS, 2, DIRS), jnp.float32), -0.1, 0.1)
    return jnp.concatenate([flux_all, cross_all], axis=1)


def draw_sky_flux(key, part):
    return sky_draw(key)


def truth_draw(key):
    freq_ratio = 1.0 + jnp.arange(CHANNELS, dtype=jnp.float32) / CHANNELS
    component = jnp.arange(8 * DIRS) // DIRS
    identity_part = ((component == 0) | (component == 3)).astype(jnp.float32)
    base_part = 0.4 * jax.random.normal(jax.random.fold_in(key, 18), (STATIONS, 1, 8 * DIRS), jnp.float32)
    slope_part = 0.2 * jax.random.normal(jax.random.fold_in(key, 19), (STATIONS, 1, 8 * DIRS), jnp.float32)
    return identity_part + base_part + slope_part * (freq_ratio - 1.5)[None, :, None]


def draw_jones_init(key, part):
    shape_all = (STATIONS, CHANNELS, 8 * DIRS)
    noise_part = 0.25 * jax.random.normal(jax.random.fold_in(key, 20), shape_all, jnp.float32)
    return jnp.clip(truth_draw(key) + noise_part, -2.0, 2.0)


def split_parts_drawn(block_jones):
    station_count = block_jones.shape[0]
    chan_count = block_jones.shape[1]
    shaped = block_jones.reshape(station_count, chan_count, 2, 2, 2, DIRS)
    shaped = jnp.transpose(shaped, (2, 1, 0, 3, 5, 4))
    return (shaped[0], shaped[1])


def sky_parts_drawn(sky_flux):
    flux_xx = sky_flux[:, 0]
    flux_yy = sky_flux[:, 1]
    cross_re = sky_flux[:, 2]
    cross_im = sky_flux[:, 3]
    zeros_k = jnp.zeros_like(flux_xx)
    real_part = jnp.stack([jnp.stack([flux_xx, cross_re], -1), jnp.stack([cross_re, flux_yy], -1)], -2)
    imag_part = jnp.stack([jnp.stack([zeros_k, cross_im], -1), jnp.stack([-cross_im, zeros_k], -1)], -2)
    return (real_part, imag_part)


def times_sky_drawn(parts, sky_pair):
    jones_re = parts[0][..., None]
    jones_im = parts[1][..., None]
    sky_re = sky_pair[0][:, None, None]
    sky_im = sky_pair[1][:, None, None]
    return (jnp.sum(jones_re * sky_re - jones_im * sky_im, axis=-2), jnp.sum(jones_re * sky_im + jones_im * sky_re, axis=-2))


def phase_angles_drawn(theta_side, freq_ratio):
    slot_count = theta_side.shape[0]
    shaped = jnp.transpose(theta_side.reshape(slot_count, DIRS, BLOCK), (0, 2, 1))
    angle_all = freq_ratio[:, None, None, None] * shaped[None]
    angle_all = angle_all[:, :, :, None, :, None]
    return (jnp.cos(angle_all), jnp.sin(angle_all))


def rotate_flat_drawn(parts, cosines, sines):
    part_re = parts[0][:, None]
    part_im = parts[1][:, None]
    out_re = cosines * part_re - sines * part_im
    out_im = cosines * part_im + sines * part_re
    chan_count = out_re.shape[0]
    slot_count = out_re.shape[1]
    return (out_re.reshape(chan_count, slot_count, 2 * BLOCK, 2 * DIRS), out_im.reshape(chan_count, slot_count, 2 * BLOCK, 2 * DIRS))


def draw_visibility(key, part):
    true_jones = truth_draw(key)
    sky_pair = sky_parts_drawn(sky_draw(key))
    phase_all = phase_draw(key)
    pair_list = pair_draw(key)
    row_table, col_table = table_pairs(STATIONS // BLOCK)
    row_of = jnp.asarray(row_table)[pair_list]
    col_of = jnp.asarray(col_table)[pair_list]
    freq_ratio = 1.0 + jnp.arange(CHANNELS, dtype=jnp.float32) / CHANNELS
    noise_key = jax.random.fold_in(key, 22)
    highest = lax.Precision.HIGHEST

    def one_tile(tile_inputs):
        tile_index, theta_tile, row_block, col_block = tile_inputs
        row_jones = lax.dynamic_slice_in_dim(true_jones, row_block * BLOCK, BLOCK, 0)
        col_jones = lax.dynamic_slice_in_dim(true_jones, col_block * BLOCK, BLOCK, 0)
        row_sky = times_sky_drawn(split_parts_drawn(row_jones), sky_pair)
        col_parts = split_parts_drawn(col_jones)
        cos_row, sin_row = phase_angles_drawn(theta_tile[:, 0], freq_ratio)
        cos_col, sin_col = phase_angles_drawn(theta_tile[:, 1], freq_ratio)
        left_re, left_im = rotate_flat_drawn(row_sky, cos_row, sin_row)
        conj_re, conj_im = rotate_flat_drawn(col_parts, cos_col, sin_col)
        model_re = jnp.einsum('ftpk,ftqk->ftpq', left_re, conj_re, precision=highest) + jnp.einsum('ftpk,ftqk->ftpq', left_im, conj_im, precision=highest)
        model_im = jnp.einsum('ftpk,ftqk->ftpq', left_im, conj_re, precision=highest) - jnp.einsum('ftpk,ftqk->ftpq', left_re, conj_im, precision=highest)
        clean_model = jnp.stack([model_re, model_im], 2)
        tile_key = jax.random.fold_in(noise_key, tile_index)
        noise_part = 0.3 * jax.random.normal(tile_key, clean_model.shape, jnp.float32)
        return jnp.clip(clean_model + noise_part, -4.0, 4.0).astype(jnp.bfloat16)
    return lax.map(one_tile, (jnp.arange(TILES), phase_all, row_of, col_of))


def place_ends(values, rng, least, top_value):
    spot = [jax.random.randint(jax.random.fold_in(rng, axis), (), 0, length) for axis, length in enumerate(values.shape)]
    longest = values.shape.index(max(values.shape))
    neighbour = spot[:longest] + [(spot[longest] + 1) % values.shape[longest]] + spot[longest + 1:]
    return values.at[tuple(spot)].set(least).at[tuple(neighbour)].set(top_value)


def steps_of(rng, shape, cuts, smallest, high):
    factor_of, own = 1.0, jax.random.fold_in(rng, 6)
    for position, blocks in cuts:
        draws = jnp.exp(jax.random.uniform(jax.random.fold_in(own, position), (blocks,), jnp.float32, smallest / len(cuts), high / len(cuts)))
        factor_of = factor_of * jnp.repeat(draws, shape[position] // blocks).reshape([-1 if axis == position else 1 for axis in range(len(shape))])
    return factor_of


def scatter_about(own_key, dims, spread, most, cuts=(), kind=jnp.bfloat16):
    gain = steps_of(own_key, dims, cuts, -0.22, 0.18) if cuts else 1.0
    drawn = jax.random.normal(own_key, dims, jnp.float32) * spread * gain
    return jnp.minimum(jnp.maximum(drawn, -most), most).astype(kind)


def setup_inputs(seed: int = 0) -> dict:
    splits = jax.random.split(jax.random.key(seed), 10)
    return {
        "jones_init": draw_jones_init(jax.random.fold_in(splits[9], 71), 0),
        "dual_init": scatter_about(splits[1], (STATIONS, CHANNELS, JW), 0.2, 1.2, ((0, 8), (1, 4)), jnp.float32),
        "penalty": jnp.clip(jnp.exp(jax.random.uniform(splits[2], (DIRS,), jnp.float32, math.log(0.5), math.log(5.0))), 0.5, 5.0),
        "sky_flux": draw_sky_flux(jax.random.fold_in(splits[9], 71), 0),
        "visibility": draw_visibility(jax.random.fold_in(splits[9], 71), 0),
        "phases": draw_phases(jax.random.fold_in(splits[9], 71), 0),
        "pair_ids": draw_pair_ids(jax.random.fold_in(splits[9], 71), 0),
        "counts": draw_counts(jax.random.fold_in(splits[9], 71), 0),
        "slot_flags": place_ends((jax.random.randint(splits[8], (TILES, TIME), 0, 8) < 7).astype(jnp.int32), jax.random.fold_in(splits[8], 1), 0, 1),
    }


STEP_SCALE = 0.3
FULL_PRECISION = lax.Precision.HIGHEST

def pair_tables(block_count):
    row_list = []
    col_list = []
    for row_block in range(block_count):
        for col_block in range(row_block, block_count):
            row_list.append(row_block)
            col_list.append(col_block)
    return (np.array(row_list, np.int32), np.array(col_list, np.int32))

def split_parts(block_jones):
    station_count = block_jones.shape[0]
    chan_count = block_jones.shape[1]
    shaped = block_jones.reshape(station_count, chan_count, 2, 2, 2, DIRS)
    shaped = jnp.transpose(shaped, (2, 1, 0, 3, 5, 4))
    return (shaped[0], shaped[1])

def sky_parts(sky_flux):
    flux_xx = sky_flux[:, 0]
    flux_yy = sky_flux[:, 1]
    cross_re = sky_flux[:, 2]
    cross_im = sky_flux[:, 3]
    zeros_k = jnp.zeros_like(flux_xx)
    real_part = jnp.stack([jnp.stack([flux_xx, cross_re], -1), jnp.stack([cross_re, flux_yy], -1)], -2)
    imag_part = jnp.stack([jnp.stack([zeros_k, cross_im], -1), jnp.stack([-cross_im, zeros_k], -1)], -2)
    return (real_part, imag_part)

def times_sky(parts, sky_pair):
    jones_re = parts[0][..., None]
    jones_im = parts[1][..., None]
    sky_re = sky_pair[0][:, None, None]
    sky_im = sky_pair[1][:, None, None]
    out_re = lax.optimization_barrier(jnp.sum(jones_re * sky_re - jones_im * sky_im, axis=-2))
    out_im = lax.optimization_barrier(jnp.sum(jones_re * sky_im + jones_im * sky_re, axis=-2))
    return (out_re, out_im)

def phase_angles(theta_side, freq_ratio):
    slot_count = theta_side.shape[0]
    shaped = jnp.transpose(theta_side.reshape(slot_count, DIRS, BLOCK), (0, 2, 1))
    angle_all = freq_ratio[:, None, None, None] * shaped[None]
    angle_all = angle_all[:, :, :, None, :, None]
    return (jnp.cos(angle_all), jnp.sin(angle_all))

def rotate_flat(parts, cosines, sines):
    part_re = parts[0][:, None]
    part_im = parts[1][:, None]
    out_re = cosines * part_re - sines * part_im
    out_im = cosines * part_im + sines * part_re
    chan_count = out_re.shape[0]
    slot_count = out_re.shape[1]
    return (out_re.reshape(chan_count, slot_count, 2 * BLOCK, 2 * DIRS), out_im.reshape(chan_count, slot_count, 2 * BLOCK, 2 * DIRS))

def unrotate(product, cosines, sines):
    chan_count = product.shape[0]
    slot_count = product.shape[1]
    shaped = product.reshape(chan_count, slot_count, BLOCK, 2, 2, DIRS, 2)
    neg_re = shaped[:, :, :, :, 0]
    neg_im = shaped[:, :, :, :, 1]
    grad_re = -lax.optimization_barrier(jnp.sum(neg_re * cosines + neg_im * sines, axis=1))
    grad_im = -lax.optimization_barrier(jnp.sum(neg_im * cosines - neg_re * sines, axis=1))
    both_parts = jnp.transpose(jnp.stack([grad_re, grad_im], 0), (2, 1, 0, 3, 5, 4))
    return both_parts.reshape(BLOCK, chan_count, 8 * DIRS)

def power_rows(parts):
    power = lax.optimization_barrier(jnp.sum(parts[0] * parts[0] + parts[1] * parts[1], axis=2))
    power = jnp.transpose(power, (1, 0, 3, 2))
    return power.reshape(power.shape[0], -1)

def slot_terms(vis_part, weights, theta_part, freq_ratio, row_sky, col_sky, col_parts, mask_wide):
    cos_row, sin_row = phase_angles(theta_part[:, 0], freq_ratio)
    cos_col, sin_col = phase_angles(theta_part[:, 1], freq_ratio)
    left_re, left_im = rotate_flat(row_sky, cos_row, sin_row)
    right_re, right_im = rotate_flat(col_sky, cos_col, sin_col)
    conj_re, conj_im = rotate_flat(col_parts, cos_col, sin_col)
    left_re = left_re.astype(jnp.bfloat16)
    left_im = left_im.astype(jnp.bfloat16)
    right_re = right_re.astype(jnp.bfloat16)
    right_im = right_im.astype(jnp.bfloat16)
    conj_re = conj_re.astype(jnp.bfloat16)
    conj_im = conj_im.astype(jnp.bfloat16)
    left_side = jnp.concatenate([left_re, left_im], -1).astype(jnp.float32)
    model_rhs = jnp.stack([jnp.concatenate([conj_re, conj_im], -1), jnp.concatenate([-conj_im, conj_re], -1)], 2).astype(jnp.float32)
    predicted = jnp.einsum('ftpk,ftcqk->ftcpq', left_side, model_rhs, precision=FULL_PRECISION)
    weighting = weights[None, :, None, None, None] * mask_wide
    residual = (weighting * (vis_part.astype(jnp.float32) - predicted)).astype(jnp.bfloat16).astype(jnp.float32)
    row_rhs = jnp.stack([jnp.concatenate([right_re, right_im], -1), jnp.concatenate([-right_im, right_re], -1)], 2).astype(jnp.float32)
    col_rhs = jnp.stack([jnp.concatenate([left_re, left_im], -1), jnp.concatenate([left_im, -left_re], -1)], 2).astype(jnp.float32)
    row_out = jnp.einsum('ftcpq,ftcqk->ftpk', residual, row_rhs, precision=FULL_PRECISION)
    col_out = jnp.einsum('ftcpq,ftcpk->ftqk', residual, col_rhs, precision=FULL_PRECISION)
    return (unrotate(row_out, cos_row, sin_row), unrotate(col_out, cos_col, sin_col))

def tile_terms(full_jones, sky_pair, freq_ratio, tables, vis_tile, theta_tile, pair_id, kept_slots, flag_row):
    pair_range = jnp.arange(tables[0].shape[0])
    row_block = jnp.sum(jnp.where(pair_range == pair_id, tables[0], 0)).astype(jnp.int32)
    col_block = jnp.sum(jnp.where(pair_range == pair_id, tables[1], 0)).astype(jnp.int32)
    row_jones = lax.dynamic_slice_in_dim(full_jones, row_block * BLOCK, BLOCK, 0)
    col_jones = lax.dynamic_slice_in_dim(full_jones, col_block * BLOCK, BLOCK, 0)
    row_sky = times_sky(split_parts(row_jones), sky_pair)
    col_parts = split_parts(col_jones)
    col_sky = times_sky(col_parts, sky_pair)
    station_rank = jnp.arange(BLOCK)
    strict = (station_rank[:, None] < station_rank[None, :]) | (row_block != col_block)
    pair_mask = strict.astype(jnp.float32)
    mask_wide = jnp.broadcast_to(pair_mask[:, None, :, None], (BLOCK, 2, BLOCK, 2)).reshape(2 * BLOCK, 2 * BLOCK)
    weights = flag_row.astype(jnp.float32) * (jnp.arange(TIME) < kept_slots).astype(jnp.float32)
    samples = jnp.sum(weights)
    row_grad, col_grad = slot_terms(vis_tile, weights, theta_tile, freq_ratio, row_sky, col_sky, col_parts, mask_wide)
    row_curv = samples * jnp.dot(pair_mask, power_rows(col_sky), precision=FULL_PRECISION)
    col_curv = samples * jnp.dot(pair_mask.T, power_rows(row_sky), precision=FULL_PRECISION)
    chan_count = full_jones.shape[1]
    return (row_block, col_block, row_grad, col_grad, row_curv.reshape(BLOCK, chan_count, 2 * DIRS), col_curv.reshape(BLOCK, chan_count, 2 * DIRS))

def add_block(total, start, piece):
    current = lax.dynamic_slice_in_dim(total, start, piece.shape[0], 0)
    return lax.dynamic_update_slice_in_dim(total, current + piece, start, 0)

def data_terms(full_jones, sky_pair, freq_ratio, tables, visibility, phases, pair_ids, counts, slot_flags):
    station_count = full_jones.shape[0]
    chan_count = full_jones.shape[1]
    grad_zero = jnp.zeros((station_count, chan_count, 8 * DIRS), jnp.float32)
    curv_zero = jnp.zeros((station_count, chan_count, 2 * DIRS), jnp.float32)

    def add_tile(carry, tile_inputs):
        grad_sum, curv_sum = carry
        vis_tile, theta_tile, pair_id, kept_slots, flag_row = tile_inputs
        row_block, col_block, row_grad, col_grad, row_curv, col_curv = tile_terms(full_jones, sky_pair, freq_ratio, tables, vis_tile, theta_tile, pair_id, kept_slots, flag_row)
        grad_sum = add_block(grad_sum, row_block * BLOCK, row_grad)
        grad_sum = add_block(grad_sum, col_block * BLOCK, col_grad)
        curv_sum = add_block(curv_sum, row_block * BLOCK, row_curv)
        curv_sum = add_block(curv_sum, col_block * BLOCK, col_curv)
        return ((grad_sum, curv_sum), None)
    totals, unused = lax.scan(add_tile, (grad_zero, curv_zero), (visibility, phases, pair_ids, counts, slot_flags))
    return totals

def cosine_basis(chan_total):
    middle = jnp.arange(chan_total, dtype=jnp.float32) + 0.5
    degree = jnp.arange(NPOLY, dtype=jnp.float32)
    normalizer = jnp.sqrt(jnp.where(degree == 0, 1.0, 2.0) / chan_total)
    return jnp.cos(jnp.pi * middle[:, None] * degree[None, :] / chan_total) * normalizer[None, :]

def project(values_all, poly_basis):
    return lax.optimization_barrier(jnp.sum(poly_basis[None, :, :, None] * values_all[:, :, None, :], axis=1))

def expand(coefficients, poly_basis):
    return lax.optimization_barrier(jnp.sum(poly_basis[None, :, :, None] * coefficients[:, None, :, :], axis=2))

def jacobi(jones_now, duals_now, gradient, curvature, penalty_full, target):
    divisor = jnp.tile(curvature, (1, 1, 4)) + 0.5 * penalty_full
    return jones_now - STEP_SCALE * (gradient + 0.5 * penalty_full * (jones_now - target) + 0.5 * duals_now) / divisor

def reference(jones_init, dual_init, penalty, sky_flux, visibility, phases, pair_ids, counts, slot_flags):
    freq_ratio = 1.0 + jnp.arange(CHANNELS, dtype=jnp.float32) / CHANNELS
    poly_basis = cosine_basis(CHANNELS)
    penalty_full = jnp.tile(penalty, 8)
    sky_pair = sky_parts(sky_flux)
    row_table, col_table = pair_tables(STATIONS // BLOCK)
    tables = (jnp.asarray(row_table), jnp.asarray(col_table))
    jones_now = jones_init
    duals_now = dual_init
    center = project(jones_now + duals_now / penalty_full, poly_basis)
    for outer_round in range(ITERS):
        target = expand(center, poly_basis)
        for inner_round in range(GSTEPS):
            gradient, curvature = data_terms(jones_now, sky_pair, freq_ratio, tables, visibility, phases, pair_ids, counts, slot_flags)
            jones_now = jacobi(jones_now, duals_now, gradient, curvature, penalty_full, target)
        center = project(jones_now + duals_now / penalty_full, poly_basis)
        duals_now = duals_now + penalty_full * (jones_now - expand(center, poly_basis))
    return (jones_now, duals_now, center)
```

```python
import jax
import jax.numpy as jnp
import numpy as np
from jax import lax
from jax.experimental import pallas as pl
from jax.experimental.pallas import tpu as pltpu
from jax.sharding import PartitionSpec as P

STATIONS = 512
DIRS = 16
BLOCK = 64
TIME = 8
NPOLY = 3
ITERS = 2


STEP_SCALE = 0.3
FULL_PRECISION = lax.Precision.HIGHEST


def pair_tables(block_count):
    row_list = []
    col_list = []
    for row_block in range(block_count):
        for col_block in range(row_block, block_count):
            row_list.append(row_block)
            col_list.append(col_block)
    return (np.array(row_list, np.int32), np.array(col_list, np.int32))


def split_parts(block_jones):
    station_count = block_jones.shape[0]
    chan_count = block_jones.shape[1]
    shaped = block_jones.reshape(station_count, chan_count, 2, 2, 2, DIRS)
    shaped = jnp.transpose(shaped, (2, 1, 0, 3, 5, 4))
    return (shaped[0], shaped[1])


def sky_parts(sky_flux):
    flux_xx = sky_flux[:, 0]
    flux_yy = sky_flux[:, 1]
    cross_re = sky_flux[:, 2]
    cross_im = sky_flux[:, 3]
    zeros_k = jnp.zeros_like(flux_xx)
    real_part = jnp.stack(
        [jnp.stack([flux_xx, cross_re], -1), jnp.stack([cross_re, flux_yy], -1)], -2
    )
    imag_part = jnp.stack(
        [jnp.stack([zeros_k, cross_im], -1), jnp.stack([-cross_im, zeros_k], -1)], -2
    )
    return (real_part, imag_part)


def times_sky(parts, sky_pair):
    jones_re = parts[0][..., None]
    jones_im = parts[1][..., None]
    sky_re = sky_pair[0][:, None, None]
    sky_im = sky_pair[1][:, None, None]
    out_re = jnp.sum(jones_re * sky_re - jones_im * sky_im, axis=-2)
    out_im = jnp.sum(jones_re * sky_im + jones_im * sky_re, axis=-2)
    return (out_re, out_im)


def phase_angles(theta_side, freq_ratio):
    slot_count = theta_side.shape[0]
    shaped = jnp.transpose(theta_side.reshape(slot_count, DIRS, BLOCK), (0, 2, 1))
    angle_all = freq_ratio[:, None, None, None] * shaped[None]
    angle_all = angle_all[:, :, :, None, :, None]
    return (jnp.cos(angle_all), jnp.sin(angle_all))


def rotate_flat(parts, cosines, sines):
    part_re = parts[0][:, None]
    part_im = parts[1][:, None]
    out_re = cosines * part_re - sines * part_im
    out_im = cosines * part_im + sines * part_re
    chan_count = out_re.shape[0]
    slot_count = out_re.shape[1]
    return (
        out_re.reshape(chan_count, slot_count, 2 * BLOCK, 2 * DIRS).astype(jnp.bfloat16),
        out_im.reshape(chan_count, slot_count, 2 * BLOCK, 2 * DIRS).astype(jnp.bfloat16),
    )


def unrotate(product, cosines, sines):
    chan_count = product.shape[0]
    slot_count = product.shape[1]
    shaped = product.reshape(chan_count, slot_count, BLOCK, 2, 2, DIRS, 2)
    neg_re = shaped[:, :, :, :, 0]
    neg_im = shaped[:, :, :, :, 1]
    grad_re = -jnp.sum(neg_re * cosines + neg_im * sines, axis=1)
    grad_im = -jnp.sum(neg_im * cosines - neg_re * sines, axis=1)
    both_parts = jnp.transpose(jnp.stack([grad_re, grad_im], 0), (2, 1, 0, 3, 5, 4))
    return both_parts.reshape(BLOCK, chan_count, 8 * DIRS)


def power_rows(parts):
    power = jnp.sum(parts[0] * parts[0] + parts[1] * parts[1], axis=2)
    power = jnp.transpose(power, (1, 0, 3, 2))
    return power.reshape(power.shape[0], -1)


def slot_terms(vis_part, weights, theta_part, freq_ratio, row_sky, col_sky, col_parts, mask_wide):
    cos_row, sin_row = phase_angles(theta_part[:, 0], freq_ratio)
    cos_col, sin_col = phase_angles(theta_part[:, 1], freq_ratio)
    left_re, left_im = rotate_flat(row_sky, cos_row, sin_row)
    right_re, right_im = rotate_flat(col_sky, cos_col, sin_col)
    conj_re, conj_im = rotate_flat(col_parts, cos_col, sin_col)
    left_side = jnp.concatenate([left_re, left_im], -1)
    model_rhs = jnp.stack(
        [jnp.concatenate([conj_re, conj_im], -1), jnp.concatenate([-conj_im, conj_re], -1)], 2
    )
    predicted = jnp.einsum(
        "ftpk,ftcqk->ftcpq", left_side, model_rhs, preferred_element_type=jnp.float32
    )
    weighting = weights[None, :, None, None, None] * mask_wide
    residual = (weighting * (vis_part.astype(jnp.float32) - predicted)).astype(jnp.bfloat16)
    row_rhs = jnp.stack(
        [jnp.concatenate([right_re, right_im], -1), jnp.concatenate([-right_im, right_re], -1)], 2
    )
    col_rhs = jnp.stack(
        [jnp.concatenate([left_re, left_im], -1), jnp.concatenate([left_im, -left_re], -1)], 2
    )
    row_out = jnp.einsum("ftcpq,ftcqk->ftpk", residual, row_rhs, preferred_element_type=jnp.float32)
    col_out = jnp.einsum("ftcpq,ftcpk->ftqk", residual, col_rhs, preferred_element_type=jnp.float32)
    return (unrotate(row_out, cos_row, sin_row), unrotate(col_out, cos_col, sin_col))


def tile_terms(
    full_jones, sky_pair, freq_ratio, tables, vis_tile, theta_tile, pair_id, kept_slots, flag_row
):
    pair_range = jnp.arange(tables[0].shape[0])
    row_block = jnp.sum(jnp.where(pair_range == pair_id, tables[0], 0)).astype(jnp.int32)
    col_block = jnp.sum(jnp.where(pair_range == pair_id, tables[1], 0)).astype(jnp.int32)
    row_jones = lax.dynamic_slice_in_dim(full_jones, row_block * BLOCK, BLOCK, 0)
    col_jones = lax.dynamic_slice_in_dim(full_jones, col_block * BLOCK, BLOCK, 0)
    row_sky = times_sky(split_parts(row_jones), sky_pair)
    col_parts = split_parts(col_jones)
    col_sky = times_sky(col_parts, sky_pair)
    station_rank = jnp.arange(BLOCK)
    strict = (station_rank[:, None] < station_rank[None, :]) | (row_block != col_block)
    pair_mask = strict.astype(jnp.float32)
    mask_wide = jnp.broadcast_to(pair_mask[:, None, :, None], (BLOCK, 2, BLOCK, 2)).reshape(
        2 * BLOCK, 2 * BLOCK
    )
    weights = flag_row.astype(jnp.float32) * (jnp.arange(TIME) < kept_slots).astype(jnp.float32)
    samples = jnp.sum(weights)
    chan_count = full_jones.shape[1]
    row_grad, col_grad = slot_terms(
        vis_tile, weights, theta_tile, freq_ratio, row_sky, col_sky, col_parts, mask_wide
    )
    row_curv = samples * jnp.dot(pair_mask, power_rows(col_sky), precision=FULL_PRECISION)
    col_curv = samples * jnp.dot(pair_mask.T, power_rows(row_sky), precision=FULL_PRECISION)
    return (
        row_block,
        col_block,
        row_grad,
        col_grad,
        row_curv.reshape(BLOCK, chan_count, 2 * DIRS),
        col_curv.reshape(BLOCK, chan_count, 2 * DIRS),
    )


def add_block(total, start, piece):
    current = lax.dynamic_slice_in_dim(total, start, piece.shape[0], 0)
    return lax.dynamic_update_slice_in_dim(total, current + piece, start, 0)


def data_terms(
    full_jones, sky_pair, freq_ratio, tables, visibility, phases, pair_ids, counts, slot_flags
):
    station_count = full_jones.shape[0]
    chan_count = full_jones.shape[1]
    grad_zero = jnp.zeros((station_count, chan_count, 8 * DIRS), jnp.float32)
    curv_zero = jnp.zeros((station_count, chan_count, 2 * DIRS), jnp.float32)

    def add_tile(carry, tile_inputs):
        grad_sum, curv_sum = carry
        vis_tile, theta_tile, pair_id, kept_slots, flag_row = tile_inputs
        row_block, col_block, row_grad, col_grad, row_curv, col_curv = tile_terms(
            full_jones,
            sky_pair,
            freq_ratio,
            tables,
            vis_tile,
            theta_tile,
            pair_id,
            kept_slots,
            flag_row,
        )
        grad_sum = add_block(grad_sum, row_block * BLOCK, row_grad)
        grad_sum = add_block(grad_sum, col_block * BLOCK, col_grad)
        curv_sum = add_block(curv_sum, row_block * BLOCK, row_curv)
        curv_sum = add_block(curv_sum, col_block * BLOCK, col_curv)
        return ((grad_sum, curv_sum), None)

    totals, unused = lax.scan(
        add_tile, (grad_zero, curv_zero), (visibility, phases, pair_ids, counts, slot_flags)
    )
    return totals


def cosine_basis(chan_total):
    middle = jnp.arange(chan_total, dtype=jnp.float32) + 0.5
    degree = jnp.arange(NPOLY, dtype=jnp.float32)
    normalizer = jnp.sqrt(jnp.where(degree == 0, 1.0, 2.0) / chan_total)
    return jnp.cos(jnp.pi * middle[:, None] * degree[None, :] / chan_total) * normalizer[None, :]


def project(values_all, poly_basis):
    return jnp.sum(poly_basis[None, :, :, None] * values_all[:, :, None, :], axis=1)


def expand(coefficients, poly_basis):
    return jnp.sum(poly_basis[None, :, :, None] * coefficients[:, None, :, :], axis=2)


def jacobi(jones_now, duals_now, gradient, curvature, penalty_full, target):
    divisor = jnp.tile(curvature, (1, 1, 4)) + 0.5 * penalty_full
    return (
        jones_now
        - STEP_SCALE
        * (gradient + 0.5 * penalty_full * (jones_now - target) + 0.5 * duals_now)
        / divisor
    )


def per_device(
    jones_init, dual_init, penalty, sky_flux, visibility, phases, pair_ids, counts, slot_flags
):
    chan_dev = jones_init.shape[1]
    chan_total = chan_dev * lax.axis_size("chan")
    chan_start = lax.axis_index("chan") * chan_dev
    freq_ratio = 1.0 + (chan_start + jnp.arange(chan_dev)).astype(jnp.float32) / chan_total
    poly_basis = lax.dynamic_slice_in_dim(cosine_basis(chan_total), chan_start, chan_dev, 0)
    penalty_full = jnp.tile(penalty, 8)
    sky_pair = sky_parts(sky_flux)
    row_table, col_table = pair_tables(STATIONS // BLOCK)
    tables = (jnp.asarray(row_table), jnp.asarray(col_table))

    def every_consensus(current, dual_now):
        return lax.psum(project(current + dual_now / penalty_full, poly_basis), "chan")

    jones_now, duals_now = (
        lax.all_gather(jones_init, "pair", axis=0, tiled=True),
        lax.all_gather(dual_init, "pair", axis=0, tiled=True),
    )
    center = every_consensus(jones_now, duals_now)
    for outer_round in range(ITERS):
        target = expand(center, poly_basis)
        grad_full, curv_full = data_terms(
            jones_now,
            sky_pair,
            freq_ratio,
            tables,
            visibility,
            phases,
            pair_ids,
            counts,
            slot_flags,
        )
        gradient, curvature = lax.psum((grad_full, curv_full), "pair")
        jones_now = jacobi(jones_now, duals_now, gradient, curvature, penalty_full, target)
        center = every_consensus(jones_now, duals_now)
        duals_now = duals_now + penalty_full * (jones_now - expand(center, poly_basis))
    own_rows = jones_init.shape[0]
    own_start = lax.axis_index("pair") * own_rows
    return (
        lax.dynamic_slice_in_dim(jones_now, own_start, own_rows, 0),
        lax.dynamic_slice_in_dim(duals_now, own_start, own_rows, 0),
        lax.dynamic_slice_in_dim(center, own_start, own_rows, 0),
    )


AUX = 8


def fused_kernel(
    dims, basis, pid_ref, cnt_ref, flag_ref, jones_ref, dual_ref, rho_ref, sky_ref, vis_ref, theta_ref,
    jones_out, dual_out, cons_out,
    jfull, dfull, vzero, vone, vtwo, terms, trig, cosr, sinr, cosc, sinc, visp, fac,
    jsend, jrecv, dsend, drecv, csend, crecv, vsend, vrecv,
):
    n, chans, outer, inner, rows, block, slots, dirs, poly, blocks = dims
    width = 8 * dirs
    part = block + AUX
    f32, bf16 = jnp.float32, jnp.bfloat16
    me = lax.axis_index("pair")
    mc = lax.axis_index("chan")
    mo, mi = me // inner, me % inner
    out_peers = [lax.rem(mo + d, outer) * inner + mi for d in range(1, outer)]
    in_peers = [mo * inner + lax.rem(mi + d, inner) for d in range(1, inner)]
    chan_peers = [lax.rem(mc + d, chans) for d in range(1, chans)]

    barrier = pltpu.get_barrier_semaphore()
    for peer in out_peers + in_peers:
        pl.semaphore_signal(barrier, inc=1, device_id={"pair": peer}, device_id_type=pl.DeviceIdType.MESH)
    for peer in chan_peers:
        pl.semaphore_signal(barrier, inc=1, device_id={"chan": peer}, device_id_type=pl.DeviceIdType.MESH)
    pl.semaphore_wait(barrier, len(out_peers) + len(in_peers) + len(chan_peers))

    pending = []

    def push(source, target, ssem, rsem, where):
        copy = pltpu.make_async_remote_copy(
            src_ref=source, dst_ref=target, send_sem=ssem, recv_sem=rsem,
            device_id=where, device_id_type=pl.DeviceIdType.MESH,
        )
        copy.start()
        pending.append(copy)

    def await_from(target, ssem, rsem, where):
        pltpu.make_async_remote_copy(
            src_ref=target, dst_ref=target, send_sem=ssem, recv_sem=rsem,
            device_id=where, device_id_type=pl.DeviceIdType.MESH,
        ).wait_recv()

    def spread(source, slot_of, ssems, rsems):
        for d, peer in enumerate(out_peers):
            push(source, slot_of(me), ssems.at[d], rsems.at[me], {"pair": peer})
        for d, peer in enumerate(in_peers):
            push(source, slot_of(me), ssems.at[outer - 1 + d], rsems.at[me], {"pair": peer})

    def relay(slot_of, ssems, rsems):
        position = outer - 1 + inner - 1
        for origin in out_peers:
            await_from(slot_of(origin), ssems.at[0], rsems.at[origin], {"pair": origin})
            for peer in in_peers:
                push(slot_of(origin), slot_of(origin), ssems.at[position], rsems.at[origin], {"pair": peer})
                position += 1

    def finish(slot_of, ssems, rsems):
        for peer in in_peers:
            for step in range(outer):
                origin = lax.rem(mo + step, outer) * inner + lax.rem(peer, inner)
                await_from(slot_of(origin), ssems.at[0], rsems.at[origin], {"pair": peer})

    def jslot(origin):
        return jfull.at[pl.ds(pl.multiple_of(origin * rows, rows), rows)]

    def dslot(origin):
        return dfull.at[pl.ds(pl.multiple_of(origin * rows, rows), rows)]

    spread(jones_ref, jslot, jsend, jrecv)
    spread(dual_ref, dslot, dsend, drecv)
    own_start = pl.multiple_of(me * rows, rows)
    jfull[pl.ds(own_start, rows), :] = jones_ref[...]
    dfull[pl.ds(own_start, rows), :] = dual_ref[...]

    def chan_spread(buffer, first, count, level):
        view = buffer.at[mc, pl.ds(first, count)]
        for d, peer in enumerate(chan_peers):
            push(view, view, vsend.at[level, d], vrecv.at[level, mc], {"chan": peer})

    def chan_finish(buffer, first, count, level):
        for peer in chan_peers:
            await_from(
                buffer.at[peer, pl.ds(first, count)], vsend.at[level, 0], vrecv.at[level, peer], {"chan": peer}
            )

    tile_k = lax.broadcasted_iota(jnp.int32, (dirs, width), 1) % dirs
    tiling = (tile_k == lax.broadcasted_iota(jnp.int32, (dirs, width), 0)).astype(f32)

    def widen(values):
        return jnp.dot(values, tiling, precision=FULL_PRECISION, preferred_element_type=f32)

    rho = widen(rho_ref[...])
    sky = widen(sky_ref[...])
    lane = lax.broadcasted_iota(jnp.int32, (1, width), 1)
    imag_lane = (lane // (4 * dirs)) % 2 == 1
    second_i = (lane // (2 * dirs)) % 2 == 1
    second_j = (lane // dirs) % 2 == 1
    sky_same = jnp.where(second_j, sky[1:2], sky[0:1])
    sky_cross = sky[2:3]
    sky_turn = jnp.where(second_j == imag_lane, sky[3:4], -sky[3:4])

    def swap(values, second, gap):
        return jnp.where(second, pltpu.roll(values, gap, 1), pltpu.roll(values, width - gap, 1))

    def swap_c(values):
        return pltpu.roll(values, 4 * dirs, 1)

    def turn(values):
        swapped = swap_c(values)
        return jnp.where(imag_lane, swapped, -swapped)

    def swap_i(values):
        return swap(values, second_i, 2 * dirs)

    def with_sky(values):
        crossed = swap(values, second_j, dirs)
        return values * sky_same + crossed * sky_cross + swap_c(crossed) * sky_turn

    def both_rows(values):
        swapped = swap_i(values)
        return jnp.concatenate(
            [jnp.where(second_i, swapped, values), jnp.where(second_i, values, swapped)], 0
        )

    def power(values):
        squared = values * values
        squared = squared + swap_c(squared)
        return squared + swap_i(squared)

    own_jones = jones_ref[...]
    own_dual = dual_ref[...]
    vzero[mc, pl.ds(0, rows), :] = own_jones + own_dual / rho
    chan_spread(vzero, 0, rows, 0)

    ratio = 1.0 + mc.astype(f32) / chans
    trig_k = lax.broadcasted_iota(jnp.int32, (2 * dirs, 2 * width), 1)
    trig_row = lax.broadcasted_iota(jnp.int32, (2 * dirs, 2 * width), 0)
    trig_tiling = ((trig_k // width) * dirs + trig_k % dirs == trig_row).astype(f32)
    for side, (cos_ref, sin_ref) in enumerate(((cosr, sinr), (cosc, sinc))):
        angle = theta_ref[:, side, :] * ratio
        cosines, sines = jnp.cos(angle), jnp.sin(angle)
        for k in range(dirs):
            trig[side, :, k, :] = cosines[:, k * block : (k + 1) * block]
            trig[side, :, dirs + k, :] = sines[:, k * block : (k + 1) * block]

        @pl.loop(0, slots)
        def expand_slot(s):
            wide = lax.dot_general(
                trig[side, s], trig_tiling, (((0,), (0,)), ((), ())),
                precision=FULL_PRECISION, preferred_element_type=f32,
            )
            cos_ref[s] = wide[:, :width]
            sin_ref[s] = wide[:, width:]

    relay(jslot, jsend, jrecv)

    two = 2 * block
    perm_row = lax.broadcasted_iota(jnp.int32, (two, two), 0)
    perm_col = lax.broadcasted_iota(jnp.int32, (two, two), 1)
    unlace = ((perm_row % block) * 2 + perm_row // block == perm_col).astype(f32).astype(bf16)
    lace = ((perm_col % block) * 2 + perm_col // block == perm_row).astype(f32).astype(bf16)

    @pl.loop(0, slots)
    def unlace_slot(s):
        for c in range(2):
            half = jnp.dot(unlace, vis_ref[2 * s + c], preferred_element_type=f32).astype(bf16)
            visp[s, :, c * two : (c + 1) * two] = jnp.dot(half, lace, preferred_element_type=f32).astype(bf16)

    pid = pid_ref[0]
    row_block = jnp.int32(0)
    row_first = jnp.int32(0)
    first = 0
    for r in range(1, blocks):
        first += blocks - r + 1
        row_block = jnp.where(pid >= first, r, row_block)
        row_first = jnp.where(pid >= first, first, row_first)
    col_block = row_block + pid - row_first
    apart = jnp.where(row_block == col_block, 0.0, 1.0).astype(f32)
    samples = jnp.float32(0.0)
    for s in range(slots):
        samples = samples + jnp.where(s < cnt_ref[0], flag_ref[0, s], 0).astype(f32)

    def load_block(buffer, which):
        wanted = jnp.full((block, width), which, jnp.int32)
        chosen = jnp.zeros((block, width), f32)
        for b in range(blocks):
            chosen = jnp.where(wanted == b, buffer[b * block : (b + 1) * block, :], chosen)
        return chosen

    upper = (lax.broadcasted_iota(jnp.int32, (two, 2 * two), 0) % block) < (
        lax.broadcasted_iota(jnp.int32, (two, 2 * two), 1) % block
    )
    half_row = lax.broadcasted_iota(jnp.int32, (two, width), 0) // block == 1
    wide_i = (lax.broadcasted_iota(jnp.int32, (two, width), 1) // (2 * dirs)) % 2 == 1
    keep_left = half_row == wide_i
    aux_row = lax.broadcasted_iota(jnp.int32, (AUX, width), 0)

    def data_terms_here(level, row_jones, col_jones):
        row_sky, col_sky = with_sky(row_jones), with_sky(col_jones)
        for spot, source in enumerate((row_sky, col_jones, col_sky)):
            fac[2 * spot] = both_rows(source)
            fac[2 * spot + 1] = both_rows(turn(source))
        row_total = samples * jnp.sum(power(row_sky), axis=0, keepdims=True)
        col_total = samples * jnp.sum(power(col_sky), axis=0, keepdims=True)
        row_id = row_block.astype(f32)
        col_id = col_block.astype(f32)
        same = samples * (1.0 - apart)
        aux_r = jnp.where(aux_row == 0, col_total, jnp.where(aux_row == 1, same, row_id))
        aux_c = jnp.where(aux_row == 0, row_total * apart, jnp.where(aux_row == 1, 0.0, col_id))

        def slot_step(s, carry):
            row_sum, col_sum = carry
            weight = jnp.where(s < cnt_ref[0], flag_ref[0, s], 0).astype(f32)
            weighting = jnp.where(upper, weight, weight * apart)
            cos_r, sin_r = cosr[s], sinr[s]
            cos_c, sin_c = cosc[s], sinc[s]
            wide = [jnp.concatenate([x, x], 0) for x in (cos_r, sin_r, cos_c, sin_c)]

            def rotated(spot, cosines, sines):
                plain, turned = fac[2 * spot], fac[2 * spot + 1]
                return (
                    cosines * plain + sines * turned,
                    cosines * turned - sines * plain,
                )

            left, left_turn = rotated(0, wide[0], wide[1])
            conj, conj_turn = rotated(1, wide[2], wide[3])
            right, right_turn = rotated(2, wide[2], wide[3])
            left_only = jnp.where(keep_left, left, 0.0).astype(bf16)
            model_rhs = jnp.concatenate([conj.astype(bf16), conj_turn.astype(bf16)], 0)
            predicted = lax.dot_general(
                left_only, model_rhs, (((1,), (1,)), ((), ())), preferred_element_type=f32
            )
            residual = (weighting * (visp[s].astype(f32) - predicted)).astype(bf16)
            row_rhs = jnp.concatenate([right.astype(bf16), right_turn.astype(bf16)], 0)
            row_out = jnp.dot(residual, row_rhs, preferred_element_type=f32)
            col_out = lax.dot_general(
                residual[:, :two], left.astype(bf16), (((0,), (0,)), ((), ())), preferred_element_type=f32
            ) - lax.dot_general(
                residual[:, two:], left_turn.astype(bf16), (((0,), (0,)), ((), ())), preferred_element_type=f32
            )
            row_pick = jnp.where(second_i, row_out[block:], row_out[:block])
            col_pick = jnp.where(second_i, col_out[block:], col_out[:block])
            row_sum = row_sum + (sin_r * turn(row_pick) - cos_r * row_pick)
            col_sum = col_sum + (sin_c * turn(col_pick) - cos_c * col_pick)
            return (row_sum, col_sum)

        zero = jnp.zeros((block, width), f32)
        row_grad, col_grad = lax.fori_loop(0, slots, slot_step, (zero, zero), unroll=UNROLL)
        terms[level, me, pl.ds(0, block), :] = row_grad
        terms[level, me, pl.ds(block, AUX), :] = aux_r
        terms[level, me, pl.ds(part, block), :] = col_grad
        terms[level, me, pl.ds(part + block, AUX), :] = aux_c

    def term_slot(level):
        return lambda origin: terms.at[level, origin]

    def gathered(level, block_id, offset, count, jones_here):
        wanted = block_id.astype(f32)
        grad = jnp.zeros((count, width), f32)
        shared = jnp.zeros((1, width), f32)
        alone = jnp.zeros((1, width), f32)
        for t in range(n):
            for side in range(2):
                base = side * part
                aux = terms[level, t, pl.ds(base + block, AUX), :]
                hit = aux[2:3] == wanted
                grad = grad + jnp.where(hit, terms[level, t, pl.ds(base + offset, count), :], 0.0)
                shared = shared + jnp.where(hit, aux[0:1], 0.0)
                alone = alone + jnp.where(hit, aux[1:2], 0.0)
        return grad, shared - alone * power(with_sky(jones_here))

    def center_of(buffer, first, count):
        values = [buffer[f, pl.ds(first, count), :] for f in range(chans)]
        return [sum(float(basis[f, m]) * values[f] for f in range(chans)) for m in range(poly)]

    mine = []
    for m in range(poly):
        coefficient = jnp.float32(basis[0, m])
        for f in range(1, chans):
            coefficient = jnp.where(mc == f, jnp.float32(basis[f, m]), coefficient)
        mine.append(coefficient)

    def expand_mine(center):
        return sum(mine[m] * center[m] for m in range(poly))

    def step_of(jones_here, duals_here, terms_here, target):
        gradient, curvature = terms_here
        return jones_here - STEP_SCALE * (
            gradient + 0.5 * rho * (jones_here - target) + 0.5 * duals_here
        ) / (curvature + 0.5 * rho)

    finish(jslot, jsend, jrecv)
    relay(dslot, dsend, drecv)
    row_jones = load_block(jfull, row_block)
    col_jones = load_block(jfull, col_block)
    data_terms_here(0, row_jones, col_jones)
    spread(terms.at[0, me], term_slot(0), csend.at[0], crecv.at[0])
    finish(dslot, dsend, drecv)
    row_dual = load_block(dfull, row_block)
    col_dual = load_block(dfull, col_block)
    vzero[mc, pl.ds(rows, block), :] = row_jones + row_dual / rho
    vzero[mc, pl.ds(rows + block, block), :] = col_jones + col_dual / rho
    chan_spread(vzero, rows, two, 1)
    chan_finish(vzero, 0, rows, 0)
    own_target = expand_mine(center_of(vzero, 0, rows))
    relay(term_slot(0), csend.at[0], crecv.at[0])
    chan_finish(vzero, rows, two, 1)
    row_target = expand_mine(center_of(vzero, rows, block))
    col_target = expand_mine(center_of(vzero, rows + block, block))
    finish(term_slot(0), csend.at[0], crecv.at[0])

    own_block = (me * rows) // block
    own_offset = pl.multiple_of((me * rows) % block, AUX)
    row_next = step_of(row_jones, row_dual, gathered(0, row_block, 0, block, row_jones), row_target)
    col_next = step_of(col_jones, col_dual, gathered(0, col_block, 0, block, col_jones), col_target)
    own_jones = step_of(
        own_jones, own_dual, gathered(0, own_block, own_offset, rows, own_jones), own_target
    )
    vone[mc] = own_jones + own_dual / rho
    chan_spread(vone, 0, rows, 2)
    data_terms_here(1, row_next, col_next)
    spread(terms.at[1, me], term_slot(1), csend.at[1], crecv.at[1])
    chan_finish(vone, 0, rows, 2)
    own_target = expand_mine(center_of(vone, 0, rows))
    own_dual = own_dual + rho * (own_jones - own_target)
    relay(term_slot(1), csend.at[1], crecv.at[1])
    finish(term_slot(1), csend.at[1], crecv.at[1])
    own_jones = step_of(
        own_jones, own_dual, gathered(1, own_block, own_offset, rows, own_jones), own_target
    )
    vtwo[mc] = own_jones + own_dual / rho
    chan_spread(vtwo, 0, rows, 3)
    jones_out[...] = own_jones
    chan_finish(vtwo, 0, rows, 3)
    center = center_of(vtwo, 0, rows)
    dual_out[...] = own_dual + rho * (own_jones - expand_mine(center))
    for m in range(poly):
        cons_out[:, m, :] = center[m]
    for copy in pending:
        copy.wait_send()


UNROLL = 2


def basis_table(chan_total):
    middle = np.arange(chan_total, dtype=np.float64) + 0.5
    degree = np.arange(NPOLY, dtype=np.float64)
    normalizer = np.sqrt(np.where(degree == 0, 1.0, 2.0) / chan_total)
    table = np.cos(np.pi * middle[:, None] * degree[None, :] / chan_total) * normalizer[None, :]
    return table.astype(np.float32)


def fused_device(
    jones_init, dual_init, penalty, sky_flux, visibility, phases, pair_ids, counts, slot_flags
):
    rows, chan_dev, width = jones_init.shape
    n, chans = lax.axis_size("pair"), lax.axis_size("chan")
    tiles, slots = visibility.shape[0], visibility.shape[2]
    two = visibility.shape[-1]
    block, dirs = two // 2, penalty.shape[0]
    if tiles != 1 or chan_dev != 1 or width != 128 or rows > block or rows % AUX:
        return per_device(
            jones_init, dual_init, penalty, sky_flux, visibility, phases, pair_ids, counts, slot_flags
        )
    inner = 2 if n % 2 == 0 else 1
    outer = n // inner
    blocks = n * rows // block
    dims = (n, chans, outer, inner, rows, block, slots, dirs, NPOLY, blocks)
    sends = outer - 1 + inner - 1 + (outer - 1) * (inner - 1)
    basis = basis_table(chans)
    part = block + AUX
    f32 = jnp.float32
    vmem = pl.BlockSpec(memory_space=pltpu.VMEM)
    smem = pl.BlockSpec(memory_space=pltpu.SMEM)
    dma = pltpu.SemaphoreType.DMA

    def body(*refs):
        fused_kernel(dims, basis, *refs)

    jones_last, duals_last, center = pl.pallas_call(
        body,
        out_shape=(
            jax.ShapeDtypeStruct((rows, width), f32),
            jax.ShapeDtypeStruct((rows, width), f32),
            jax.ShapeDtypeStruct((rows, NPOLY, width), f32),
        ),
        in_specs=[smem] * 3 + [vmem] * 6,
        out_specs=(vmem, vmem, vmem),
        scratch_shapes=[
            pltpu.VMEM((n * rows, width), f32),
            pltpu.VMEM((n * rows, width), f32),
            pltpu.VMEM((chans, rows + two, width), f32),
            pltpu.VMEM((chans, rows, width), f32),
            pltpu.VMEM((chans, rows, width), f32),
            pltpu.VMEM((ITERS, n, 2 * part, width), f32),
            pltpu.VMEM((2, slots, 2 * dirs, block), f32),
            pltpu.VMEM((slots, block, width), f32),
            pltpu.VMEM((slots, block, width), f32),
            pltpu.VMEM((slots, block, width), f32),
            pltpu.VMEM((slots, block, width), f32),
            pltpu.VMEM((slots, two, 2 * two), jnp.bfloat16),
            pltpu.VMEM((6, two, width), f32),
            dma((sends,)), dma((n,)), dma((sends,)), dma((n,)),
            dma((ITERS, sends)), dma((ITERS, n)), dma((4, chans)), dma((4, chans)),
        ],
        compiler_params=pltpu.CompilerParams(
            collective_id=0, has_side_effects=True, vmem_limit_bytes=48 * 1024 * 1024
        ),
    )(
        pair_ids,
        counts,
        slot_flags,
        jones_init.reshape(rows, width),
        dual_init.reshape(rows, width),
        penalty.reshape(1, dirs),
        sky_flux.reshape(sky_flux.shape[1], dirs),
        visibility.reshape(2 * slots, two, two),
        phases.reshape(slots, 2, phases.shape[-1]),
    )
    return (jones_last.reshape(rows, 1, width), duals_last.reshape(rows, 1, width), center)


def solution(mesh):
    in_specs = (
        P("pair", "chan", None),
        P("pair", "chan", None),
        P(),
        P("chan", None, None),
        P("pair", "chan", None, None, None, None),
        P("pair", None, None, None),
        P("pair"),
        P("pair"),
        P("pair", None),
    )
    out_specs = (P("pair", "chan", None), P("pair", "chan", None), P("pair", None, None))
    return jax.shard_map(
        fused_device, mesh=mesh, in_specs=in_specs, out_specs=out_specs, check_vma=False
    )
```

```python
import jax
import jax.numpy as jnp
import numpy as np
from jax import lax
from jax.experimental import pallas as pl
from jax.experimental.pallas import tpu as pltpu
from jax.sharding import PartitionSpec as P

STATIONS = 512
DIRS = 16
BLOCK = 64
TIME = 8
NPOLY = 3
ITERS = 2


STEP_SCALE = 0.3
FULL_PRECISION = lax.Precision.HIGHEST


def pair_tables(block_count):
    row_list = []
    col_list = []
    for row_block in range(block_count):
        for col_block in range(row_block, block_count):
            row_list.append(row_block)
            col_list.append(col_block)
    return (np.array(row_list, np.int32), np.array(col_list, np.int32))


def split_parts(block_jones):
    station_count = block_jones.shape[0]
    chan_count = block_jones.shape[1]
    shaped = block_jones.reshape(station_count, chan_count, 2, 2, 2, DIRS)
    shaped = jnp.transpose(shaped, (2, 1, 0, 3, 5, 4))
    return (shaped[0], shaped[1])


def sky_parts(sky_flux):
    flux_xx = sky_flux[:, 0]
    flux_yy = sky_flux[:, 1]
    cross_re = sky_flux[:, 2]
    cross_im = sky_flux[:, 3]
    zeros_k = jnp.zeros_like(flux_xx)
    real_part = jnp.stack(
        [jnp.stack([flux_xx, cross_re], -1), jnp.stack([cross_re, flux_yy], -1)], -2
    )
    imag_part = jnp.stack(
        [jnp.stack([zeros_k, cross_im], -1), jnp.stack([-cross_im, zeros_k], -1)], -2
    )
    return (real_part, imag_part)


def times_sky(parts, sky_pair):
    jones_re = parts[0][..., None]
    jones_im = parts[1][..., None]
    sky_re = sky_pair[0][:, None, None]
    sky_im = sky_pair[1][:, None, None]
    out_re = jnp.sum(jones_re * sky_re - jones_im * sky_im, axis=-2)
    out_im = jnp.sum(jones_re * sky_im + jones_im * sky_re, axis=-2)
    return (out_re, out_im)


def phase_angles(theta_side, freq_ratio):
    slot_count = theta_side.shape[0]
    shaped = jnp.transpose(theta_side.reshape(slot_count, DIRS, BLOCK), (0, 2, 1))
    angle_all = freq_ratio[:, None, None, None] * shaped[None]
    angle_all = angle_all[:, :, :, None, :, None]
    return (jnp.cos(angle_all), jnp.sin(angle_all))


def rotate_flat(parts, cosines, sines):
    part_re = parts[0][:, None]
    part_im = parts[1][:, None]
    out_re = cosines * part_re - sines * part_im
    out_im = cosines * part_im + sines * part_re
    chan_count = out_re.shape[0]
    slot_count = out_re.shape[1]
    return (
        out_re.reshape(chan_count, slot_count, 2 * BLOCK, 2 * DIRS).astype(jnp.bfloat16),
        out_im.reshape(chan_count, slot_count, 2 * BLOCK, 2 * DIRS).astype(jnp.bfloat16),
    )


def unrotate(product, cosines, sines):
    chan_count = product.shape[0]
    slot_count = product.shape[1]
    shaped = product.reshape(chan_count, slot_count, BLOCK, 2, 2, DIRS, 2)
    neg_re = shaped[:, :, :, :, 0]
    neg_im = shaped[:, :, :, :, 1]
    grad_re = -jnp.sum(neg_re * cosines + neg_im * sines, axis=1)
    grad_im = -jnp.sum(neg_im * cosines - neg_re * sines, axis=1)
    both_parts = jnp.transpose(jnp.stack([grad_re, grad_im], 0), (2, 1, 0, 3, 5, 4))
    return both_parts.reshape(BLOCK, chan_count, 8 * DIRS)


def power_rows(parts):
    power = jnp.sum(parts[0] * parts[0] + parts[1] * parts[1], axis=2)
    power = jnp.transpose(power, (1, 0, 3, 2))
    return power.reshape(power.shape[0], -1)


def slot_terms(vis_part, weights, theta_part, freq_ratio, row_sky, col_sky, col_parts, mask_wide):
    cos_row, sin_row = phase_angles(theta_part[:, 0], freq_ratio)
    cos_col, sin_col = phase_angles(theta_part[:, 1], freq_ratio)
    left_re, left_im = rotate_flat(row_sky, cos_row, sin_row)
    right_re, right_im = rotate_flat(col_sky, cos_col, sin_col)
    conj_re, conj_im = rotate_flat(col_parts, cos_col, sin_col)
    left_side = jnp.concatenate([left_re, left_im], -1)
    model_rhs = jnp.stack(
        [jnp.concatenate([conj_re, conj_im], -1), jnp.concatenate([-conj_im, conj_re], -1)], 2
    )
    predicted = jnp.einsum(
        "ftpk,ftcqk->ftcpq", left_side, model_rhs, preferred_element_type=jnp.float32
    )
    weighting = weights[None, :, None, None, None] * mask_wide
    residual = (weighting * (vis_part.astype(jnp.float32) - predicted)).astype(jnp.bfloat16)
    row_rhs = jnp.stack(
        [jnp.concatenate([right_re, right_im], -1), jnp.concatenate([-right_im, right_re], -1)], 2
    )
    col_rhs = jnp.stack(
        [jnp.concatenate([left_re, left_im], -1), jnp.concatenate([left_im, -left_re], -1)], 2
    )
    row_out = jnp.einsum("ftcpq,ftcqk->ftpk", residual, row_rhs, preferred_element_type=jnp.float32)
    col_out = jnp.einsum("ftcpq,ftcpk->ftqk", residual, col_rhs, preferred_element_type=jnp.float32)
    return (unrotate(row_out, cos_row, sin_row), unrotate(col_out, cos_col, sin_col))


def tile_terms(
    full_jones, sky_pair, freq_ratio, tables, vis_tile, theta_tile, pair_id, kept_slots, flag_row
):
    pair_range = jnp.arange(tables[0].shape[0])
    row_block = jnp.sum(jnp.where(pair_range == pair_id, tables[0], 0)).astype(jnp.int32)
    col_block = jnp.sum(jnp.where(pair_range == pair_id, tables[1], 0)).astype(jnp.int32)
    row_jones = lax.dynamic_slice_in_dim(full_jones, row_block * BLOCK, BLOCK, 0)
    col_jones = lax.dynamic_slice_in_dim(full_jones, col_block * BLOCK, BLOCK, 0)
    row_sky = times_sky(split_parts(row_jones), sky_pair)
    col_parts = split_parts(col_jones)
    col_sky = times_sky(col_parts, sky_pair)
    station_rank = jnp.arange(BLOCK)
    strict = (station_rank[:, None] < station_rank[None, :]) | (row_block != col_block)
    pair_mask = strict.astype(jnp.float32)
    mask_wide = jnp.broadcast_to(pair_mask[:, None, :, None], (BLOCK, 2, BLOCK, 2)).reshape(
        2 * BLOCK, 2 * BLOCK
    )
    weights = flag_row.astype(jnp.float32) * (jnp.arange(TIME) < kept_slots).astype(jnp.float32)
    samples = jnp.sum(weights)
    chan_count = full_jones.shape[1]
    row_grad, col_grad = slot_terms(
        vis_tile, weights, theta_tile, freq_ratio, row_sky, col_sky, col_parts, mask_wide
    )
    row_curv = samples * jnp.dot(pair_mask, power_rows(col_sky), precision=FULL_PRECISION)
    col_curv = samples * jnp.dot(pair_mask.T, power_rows(row_sky), precision=FULL_PRECISION)
    return (
        row_block,
        col_block,
        row_grad,
        col_grad,
        row_curv.reshape(BLOCK, chan_count, 2 * DIRS),
        col_curv.reshape(BLOCK, chan_count, 2 * DIRS),
    )


def add_block(total, start, piece):
    current = lax.dynamic_slice_in_dim(total, start, piece.shape[0], 0)
    return lax.dynamic_update_slice_in_dim(total, current + piece, start, 0)


def data_terms(
    full_jones, sky_pair, freq_ratio, tables, visibility, phases, pair_ids, counts, slot_flags
):
    station_count = full_jones.shape[0]
    chan_count = full_jones.shape[1]
    grad_zero = jnp.zeros((station_count, chan_count, 8 * DIRS), jnp.float32)
    curv_zero = jnp.zeros((station_count, chan_count, 2 * DIRS), jnp.float32)

    def add_tile(carry, tile_inputs):
        grad_sum, curv_sum = carry
        vis_tile, theta_tile, pair_id, kept_slots, flag_row = tile_inputs
        row_block, col_block, row_grad, col_grad, row_curv, col_curv = tile_terms(
            full_jones,
            sky_pair,
            freq_ratio,
            tables,
            vis_tile,
            theta_tile,
            pair_id,
            kept_slots,
            flag_row,
        )
        grad_sum = add_block(grad_sum, row_block * BLOCK, row_grad)
        grad_sum = add_block(grad_sum, col_block * BLOCK, col_grad)
        curv_sum = add_block(curv_sum, row_block * BLOCK, row_curv)
        curv_sum = add_block(curv_sum, col_block * BLOCK, col_curv)
        return ((grad_sum, curv_sum), None)

    totals, unused = lax.scan(
        add_tile, (grad_zero, curv_zero), (visibility, phases, pair_ids, counts, slot_flags)
    )
    return totals


def cosine_basis(chan_total):
    middle = jnp.arange(chan_total, dtype=jnp.float32) + 0.5
    degree = jnp.arange(NPOLY, dtype=jnp.float32)
    normalizer = jnp.sqrt(jnp.where(degree == 0, 1.0, 2.0) / chan_total)
    return jnp.cos(jnp.pi * middle[:, None] * degree[None, :] / chan_total) * normalizer[None, :]


def project(values_all, poly_basis):
    return jnp.sum(poly_basis[None, :, :, None] * values_all[:, :, None, :], axis=1)


def expand(coefficients, poly_basis):
    return jnp.sum(poly_basis[None, :, :, None] * coefficients[:, None, :, :], axis=2)


def jacobi(jones_now, duals_now, gradient, curvature, penalty_full, target):
    divisor = jnp.tile(curvature, (1, 1, 4)) + 0.5 * penalty_full
    return (
        jones_now
        - STEP_SCALE
        * (gradient + 0.5 * penalty_full * (jones_now - target) + 0.5 * duals_now)
        / divisor
    )


def per_device(
    jones_init, dual_init, penalty, sky_flux, visibility, phases, pair_ids, counts, slot_flags
):
    chan_dev = jones_init.shape[1]
    chan_total = chan_dev * lax.axis_size("chan")
    chan_start = lax.axis_index("chan") * chan_dev
    freq_ratio = 1.0 + (chan_start + jnp.arange(chan_dev)).astype(jnp.float32) / chan_total
    poly_basis = lax.dynamic_slice_in_dim(cosine_basis(chan_total), chan_start, chan_dev, 0)
    penalty_full = jnp.tile(penalty, 8)
    sky_pair = sky_parts(sky_flux)
    row_table, col_table = pair_tables(STATIONS // BLOCK)
    tables = (jnp.asarray(row_table), jnp.asarray(col_table))

    def every_consensus(current, dual_now):
        return lax.psum(project(current + dual_now / penalty_full, poly_basis), "chan")

    jones_now, duals_now = (
        lax.all_gather(jones_init, "pair", axis=0, tiled=True),
        lax.all_gather(dual_init, "pair", axis=0, tiled=True),
    )
    center = every_consensus(jones_now, duals_now)
    for outer_round in range(ITERS):
        target = expand(center, poly_basis)
        grad_full, curv_full = data_terms(
            jones_now,
            sky_pair,
            freq_ratio,
            tables,
            visibility,
            phases,
            pair_ids,
            counts,
            slot_flags,
        )
        gradient, curvature = lax.psum((grad_full, curv_full), "pair")
        jones_now = jacobi(jones_now, duals_now, gradient, curvature, penalty_full, target)
        center = every_consensus(jones_now, duals_now)
        duals_now = duals_now + penalty_full * (jones_now - expand(center, poly_basis))
    own_rows = jones_init.shape[0]
    own_start = lax.axis_index("pair") * own_rows
    return (
        lax.dynamic_slice_in_dim(jones_now, own_start, own_rows, 0),
        lax.dynamic_slice_in_dim(duals_now, own_start, own_rows, 0),
        lax.dynamic_slice_in_dim(center, own_start, own_rows, 0),
    )


AUX = 8


def flipped(value, mask):
    bit = 1
    while bit <= mask:
        if mask & bit:
            value = value + bit * (1 - 2 * ((value // bit) % 2))
        bit *= 2
    return value


def fused_kernel(
    dims, basis, pid_ref, cnt_ref, flag_ref, jones_hbm, dual_hbm, rho_ref, sky_ref, vis_hbm, theta_hbm,
    jones_out, dual_out, cons_out,
    jfull, dfull, vzero, vone, vtwo, terms, last, trig, cosr, sinr, cosc, sinc, visp, fac,
    vis_ref, theta_ref, sums, inbox, jsend, jrecv, dsend, drecv, csend, crecv, vsend, vrecv, rsend, rrecv, local,
):
    n, chans, outer, inner, rows, block, slots, dirs, poly, blocks = dims
    width = 8 * dirs
    part = block + AUX
    f32, bf16 = jnp.float32, jnp.bfloat16
    me = lax.axis_index("pair")
    mc = lax.axis_index("chan")
    mo, mi = me // inner, me % inner
    if outer & (outer - 1):
        out_rows = [lax.rem(mo + d, outer) for d in range(1, outer)]
    else:
        out_rows = [flipped(mo, d) for d in range(1, outer)]
    out_peers = [o * inner + mi for o in out_rows]
    in_peers = [mo * inner + lax.rem(mi + d, inner) for d in range(1, inner)]
    chan_peers = [lax.rem(mc + d, chans) for d in range(1, chans)]

    barrier = pltpu.get_barrier_semaphore()
    for peer in out_peers + in_peers:
        pl.semaphore_signal(barrier, inc=1, device_id={"pair": peer}, device_id_type=pl.DeviceIdType.MESH)
    for peer in chan_peers:
        pl.semaphore_signal(barrier, inc=1, device_id={"chan": peer}, device_id_type=pl.DeviceIdType.MESH)
    own_start = pl.multiple_of(me * rows, rows)
    own_jref = jfull.at[pl.ds(own_start, rows)]
    own_dref = dfull.at[pl.ds(own_start, rows)]
    fetches = [
        pltpu.make_async_copy(jones_hbm, own_jref, local.at[0]),
        pltpu.make_async_copy(theta_hbm, theta_ref, local.at[1]),
        pltpu.make_async_copy(dual_hbm, own_dref, local.at[2]),
        pltpu.make_async_copy(vis_hbm, vis_ref, local.at[3]),
    ]
    for fetch in fetches:
        fetch.start()
    pl.semaphore_wait(barrier, len(out_peers) + len(in_peers) + len(chan_peers))

    pending = []

    def push(source, target, ssem, rsem, where):
        copy = pltpu.make_async_remote_copy(
            src_ref=source, dst_ref=target, send_sem=ssem, recv_sem=rsem,
            device_id=where, device_id_type=pl.DeviceIdType.MESH,
        )
        copy.start()
        pending.append(copy)

    def await_from(target, ssem, rsem, where):
        pltpu.make_async_remote_copy(
            src_ref=target, dst_ref=target, send_sem=ssem, recv_sem=rsem,
            device_id=where, device_id_type=pl.DeviceIdType.MESH,
        ).wait_recv()

    def spread(source, slot_of, ssems, rsems):
        for d, peer in enumerate(out_peers):
            push(source, slot_of(me), ssems.at[d], rsems.at[me], {"pair": peer})
        for d, peer in enumerate(in_peers):
            push(source, slot_of(me), ssems.at[outer - 1 + d], rsems.at[me], {"pair": peer})

    def relay(slot_of, ssems, rsems):
        position = outer - 1 + inner - 1
        for origin in out_peers:
            await_from(slot_of(origin), ssems.at[0], rsems.at[origin], {"pair": origin})
            for peer in in_peers:
                push(slot_of(origin), slot_of(origin), ssems.at[position], rsems.at[origin], {"pair": peer})
                position += 1

    def late_origins():
        return [o * inner + lax.rem(peer, inner) for peer in in_peers for o in [mo] + out_rows]

    def await_late(origin, slot_of, ssems, rsems):
        await_from(slot_of(origin), ssems.at[0], rsems.at[origin], {"pair": in_peers[0]})

    def finish(slot_of, ssems, rsems):
        for origin in late_origins():
            await_late(origin, slot_of, ssems, rsems)

    def jslot(origin):
        return jfull.at[pl.ds(pl.multiple_of(origin * rows, rows), rows)]

    def dslot(origin):
        return dfull.at[pl.ds(pl.multiple_of(origin * rows, rows), rows)]

    fetches[0].wait()
    spread(own_jref, jslot, jsend, jrecv)

    def chan_spread(buffer, first, count, level):
        view = buffer.at[mc, pl.ds(first, count)]
        for d, peer in enumerate(chan_peers):
            push(view, view, vsend.at[level, d], vrecv.at[level, mc], {"chan": peer})

    def chan_finish(buffer, first, count, level):
        for peer in chan_peers:
            await_from(
                buffer.at[peer, pl.ds(first, count)], vsend.at[level, 0], vrecv.at[level, peer], {"chan": peer}
            )

    tile_k = lax.broadcasted_iota(jnp.int32, (dirs, width), 1) % dirs
    tiling = (tile_k == lax.broadcasted_iota(jnp.int32, (dirs, width), 0)).astype(f32)

    def widen(values):
        return jnp.dot(values, tiling, precision=FULL_PRECISION, preferred_element_type=f32)

    rho = widen(rho_ref[...])
    sky = widen(sky_ref[...])
    lane = lax.broadcasted_iota(jnp.int32, (1, width), 1)
    imag_lane = (lane // (4 * dirs)) % 2 == 1
    second_i = (lane // (2 * dirs)) % 2 == 1
    second_j = (lane // dirs) % 2 == 1
    sky_same = jnp.where(second_j, sky[1:2], sky[0:1])
    sky_cross = sky[2:3]
    sky_turn = jnp.where(second_j == imag_lane, sky[3:4], -sky[3:4])

    def swap(values, second, gap):
        return jnp.where(second, pltpu.roll(values, gap, 1), pltpu.roll(values, width - gap, 1))

    def swap_c(values):
        return pltpu.roll(values, 4 * dirs, 1)

    def turn(values):
        swapped = swap_c(values)
        return jnp.where(imag_lane, swapped, -swapped)

    def swap_i(values):
        return swap(values, second_i, 2 * dirs)

    def with_sky(values):
        crossed = swap(values, second_j, dirs)
        return values * sky_same + crossed * sky_cross + swap_c(crossed) * sky_turn

    def both_rows(values):
        swapped = swap_i(values)
        return jnp.concatenate(
            [jnp.where(second_i, swapped, values), jnp.where(second_i, values, swapped)], 0
        )

    def power(values):
        squared = values * values
        squared = squared + swap_c(squared)
        return squared + swap_i(squared)

    ratio = 1.0 + mc.astype(f32) / chans
    trig_k = lax.broadcasted_iota(jnp.int32, (6 * dirs, 2 * width), 1)
    trig_row = lax.broadcasted_iota(jnp.int32, (6 * dirs, 2 * width), 0) % (2 * dirs)
    trig_tiling = ((trig_k // width) * dirs + trig_k % dirs == trig_row).astype(f32).astype(bf16)
    fetches[1].wait()
    for side, (cos_ref, sin_ref) in enumerate(((cosr, sinr), (cosc, sinc))):
        angle = theta_ref[:, side, :] * ratio
        cosines, sines = jnp.cos(angle), jnp.sin(angle)
        for k in range(dirs):
            trig[side, :, k, :] = cosines[:, k * block : (k + 1) * block]
            trig[side, :, dirs + k, :] = sines[:, k * block : (k + 1) * block]

        for s in range(slots):
            exact = trig[side, s]
            high = exact.astype(bf16)
            rest = exact - high.astype(f32)
            middle = rest.astype(bf16)
            low = (rest - middle.astype(f32)).astype(bf16)
            wide = lax.dot_general(
                jnp.concatenate([high, middle, low], 0), trig_tiling, (((0,), (0,)), ((), ())),
                preferred_element_type=f32,
            )
            cos_ref[s] = wide[:, :width]
            sin_ref[s] = wide[:, width:]

        if side == 0:
            relay(jslot, jsend, jrecv)

    fetches[2].wait()
    spread(own_dref, dslot, dsend, drecv)
    own_jones = own_jref[...]
    own_dual = own_dref[...]
    vzero[mc, pl.ds(0, rows), :] = own_jones + own_dual / rho
    chan_spread(vzero, 0, rows, 0)
    fetches[3].wait()

    two = 2 * block
    perm_row = lax.broadcasted_iota(jnp.int32, (two, two), 0)
    perm_col = lax.broadcasted_iota(jnp.int32, (two, two), 1)
    unlace = ((perm_row % block) * 2 + perm_row // block == perm_col).astype(f32).astype(bf16)
    lace = ((perm_col % block) * 2 + perm_col // block == perm_row).astype(f32).astype(bf16)

    for s in range(slots):
        for c in range(2):
            half = jnp.dot(unlace, vis_ref[2 * s + c], preferred_element_type=f32).astype(bf16)
            visp[s, :, c * two : (c + 1) * two] = jnp.dot(half, lace, preferred_element_type=f32).astype(bf16)

    pid = pid_ref[0]
    row_block = jnp.int32(0)
    row_first = jnp.int32(0)
    first = 0
    for r in range(1, blocks):
        first += blocks - r + 1
        row_block = jnp.where(pid >= first, r, row_block)
        row_first = jnp.where(pid >= first, first, row_first)
    col_block = row_block + pid - row_first
    apart = jnp.where(row_block == col_block, 0.0, 1.0).astype(f32)
    samples = jnp.float32(0.0)
    for s in range(slots):
        samples = samples + jnp.where(s < cnt_ref[0], flag_ref[0, s], 0).astype(f32)

    def load_block(buffer, which):
        wanted = jnp.full((block, width), which, jnp.int32)
        chosen = jnp.zeros((block, width), f32)
        for b in range(blocks):
            chosen = jnp.where(wanted == b, buffer[b * block : (b + 1) * block, :], chosen)
        return chosen

    upper = (lax.broadcasted_iota(jnp.int32, (two, 2 * two), 0) % block) < (
        lax.broadcasted_iota(jnp.int32, (two, 2 * two), 1) % block
    )
    half_row = lax.broadcasted_iota(jnp.int32, (two, width), 0) // block == 1
    wide_i = (lax.broadcasted_iota(jnp.int32, (two, width), 1) // (2 * dirs)) % 2 == 1
    keep_left = half_row == wide_i
    aux_row = lax.broadcasted_iota(jnp.int32, (AUX, width), 0)

    def data_terms_here(row_jones, col_jones):
        row_sky, col_sky = with_sky(row_jones), with_sky(col_jones)
        for spot, source in enumerate((row_sky, col_jones, col_sky)):
            fac[2 * spot] = both_rows(source)
            fac[2 * spot + 1] = both_rows(turn(source))
        row_total = samples * jnp.sum(power(row_sky), axis=0, keepdims=True)
        col_total = samples * jnp.sum(power(col_sky), axis=0, keepdims=True)
        row_id = row_block.astype(f32)
        col_id = col_block.astype(f32)
        same = samples * (1.0 - apart)
        aux_r = jnp.where(aux_row == 0, col_total, jnp.where(aux_row == 1, same, row_id))
        aux_c = jnp.where(aux_row == 0, row_total * apart, jnp.where(aux_row == 1, 0.0, col_id))

        def slot_step(s, carry):
            row_sum, col_sum = carry
            weight = jnp.where(s < cnt_ref[0], flag_ref[0, s], 0).astype(f32)
            weighting = jnp.where(upper, weight, weight * apart)
            cos_r, sin_r = cosr[s], sinr[s]
            cos_c, sin_c = cosc[s], sinc[s]
            wide = [jnp.concatenate([x, x], 0) for x in (cos_r, sin_r, cos_c, sin_c)]

            def rotated(spot, cosines, sines):
                plain, turned = fac[2 * spot], fac[2 * spot + 1]
                return (
                    cosines * plain + sines * turned,
                    cosines * turned - sines * plain,
                )

            left, left_turn = rotated(0, wide[0], wide[1])
            conj, conj_turn = rotated(1, wide[2], wide[3])
            right, right_turn = rotated(2, wide[2], wide[3])
            left_only = jnp.where(keep_left, left, 0.0).astype(bf16)
            model_rhs = jnp.concatenate([conj.astype(bf16), conj_turn.astype(bf16)], 0)
            predicted = lax.dot_general(
                left_only, model_rhs, (((1,), (1,)), ((), ())), preferred_element_type=f32
            )
            residual = (weighting * (visp[s].astype(f32) - predicted)).astype(bf16)
            row_rhs = jnp.concatenate([right.astype(bf16), right_turn.astype(bf16)], 0)
            row_out = jnp.dot(residual, row_rhs, preferred_element_type=f32)
            col_out = lax.dot_general(
                residual[:, :two], left.astype(bf16), (((0,), (0,)), ((), ())), preferred_element_type=f32
            ) - lax.dot_general(
                residual[:, two:], left_turn.astype(bf16), (((0,), (0,)), ((), ())), preferred_element_type=f32
            )
            row_pick = jnp.where(second_i, row_out[block:], row_out[:block])
            col_pick = jnp.where(second_i, col_out[block:], col_out[:block])
            row_sum = row_sum + (sin_r * turn(row_pick) - cos_r * row_pick)
            col_sum = col_sum + (sin_c * turn(col_pick) - cos_c * col_pick)
            return (row_sum, col_sum)

        zero = jnp.zeros((block, width), f32)
        row_grad, col_grad = lax.fori_loop(0, slots, slot_step, (zero, zero), unroll=UNROLL)
        return row_grad, aux_r, col_grad, aux_c

    def term_slot(origin):
        return terms.at[origin]

    def gather_start(count):
        return (
            jnp.zeros((count, width), f32), jnp.zeros((1, width), f32), jnp.zeros((1, width), f32)
        )

    def gather_add(so_far, origin, block_id, offset, count):
        wanted = block_id.astype(f32)
        grad, shared, alone = so_far
        for side in range(2):
            base = side * part
            aux = terms[origin, pl.ds(base + block, AUX), :]
            hit = aux[2:3] == wanted
            grad = grad + jnp.where(hit, terms[origin, pl.ds(base + offset, count), :], 0.0)
            shared = shared + jnp.where(hit, aux[0:1], 0.0)
            alone = alone + jnp.where(hit, aux[1:2], 0.0)
        return grad, shared, alone

    def gather_end(so_far, jones_here):
        grad, shared, alone = so_far
        return grad, shared - alone * power(with_sky(jones_here))

    def center_of(buffer, first, count):
        values = [buffer[f, pl.ds(first, count), :] for f in range(chans)]
        return [sum(float(basis[f, m]) * values[f] for f in range(chans)) for m in range(poly)]

    mine = []
    for m in range(poly):
        coefficient = jnp.float32(basis[0, m])
        for f in range(1, chans):
            coefficient = jnp.where(mc == f, jnp.float32(basis[f, m]), coefficient)
        mine.append(coefficient)

    def expand_mine(center):
        return sum(mine[m] * center[m] for m in range(poly))

    def step_of(jones_here, duals_here, terms_here, target):
        gradient, curvature = terms_here
        return jones_here - STEP_SCALE * (
            gradient + 0.5 * rho * (jones_here - target) + 0.5 * duals_here
        ) / (curvature + 0.5 * rho)

    finish(jslot, jsend, jrecv)
    relay(dslot, dsend, drecv)
    row_jones = load_block(jfull, row_block)
    col_jones = load_block(jfull, col_block)
    row_grad, aux_r, col_grad, aux_c = data_terms_here(row_jones, col_jones)
    terms[me, pl.ds(0, block), :] = row_grad
    terms[me, pl.ds(block, AUX), :] = aux_r
    terms[me, pl.ds(part, block), :] = col_grad
    terms[me, pl.ds(part + block, AUX), :] = aux_c
    spread(terms.at[me], term_slot, csend, crecv)
    finish(dslot, dsend, drecv)
    row_dual = load_block(dfull, row_block)
    col_dual = load_block(dfull, col_block)
    vzero[mc, pl.ds(rows, block), :] = row_jones + row_dual / rho
    vzero[mc, pl.ds(rows + block, block), :] = col_jones + col_dual / rho
    chan_spread(vzero, rows, two, 1)
    relay(term_slot, csend, crecv)
    row_so = gather_start(block)
    col_so = gather_start(block)
    for origin in [me] + out_peers:
        row_so = gather_add(row_so, origin, row_block, 0, block)
        col_so = gather_add(col_so, origin, col_block, 0, block)
    chan_finish(vzero, 0, rows, 0)
    chan_finish(vzero, rows, two, 1)
    own_target = expand_mine(center_of(vzero, 0, rows))
    row_target = expand_mine(center_of(vzero, rows, block))
    col_target = expand_mine(center_of(vzero, rows + block, block))
    for origin in late_origins():
        await_late(origin, term_slot, csend, crecv)
        row_so = gather_add(row_so, origin, row_block, 0, block)
        col_so = gather_add(col_so, origin, col_block, 0, block)
    row_next = step_of(row_jones, row_dual, gather_end(row_so, row_jones), row_target)
    col_next = step_of(col_jones, col_dual, gather_end(col_so, col_jones), col_target)

    row_grad, aux_r, col_grad, aux_c = data_terms_here(row_next, col_next)
    last[pl.ds(0, block), :] = row_grad
    last[pl.ds(block, block), :] = col_grad
    message = rows + AUX

    def meant_for(owner):
        owner_block = (owner * rows) // block
        offset = pl.multiple_of((owner * rows) % block, AUX)
        to_row = jnp.where(jnp.full((1, width), row_block, jnp.int32) == owner_block, 1, 0) == 1
        to_col = jnp.where(jnp.full((1, width), col_block, jnp.int32) == owner_block, 1, 0) == 1
        grad = jnp.where(to_row, last[pl.ds(offset, rows), :], 0.0) + jnp.where(
            to_col, last[pl.ds(block + offset, rows), :], 0.0
        )
        return grad, jnp.where(to_row, aux_r, 0.0) + jnp.where(to_col, aux_c, 0.0)

    for d, peer in enumerate(in_peers):
        far = lax.rem(peer, inner)
        for z, o in enumerate(out_rows + [mo]):
            spot = d * outer + z
            grad, aux = meant_for(o * inner + far)
            sums[spot, pl.ds(0, rows), :] = grad
            sums[spot, pl.ds(rows, AUX), :] = aux
            push(
                sums.at[spot], inbox.at[mi * outer + o], rsend.at[spot], rrecv.at[mi * outer + o], {"pair": peer}
            )
    base = (inner - 1) * outer
    arrivals = inner * outer
    total = None
    for z, o in enumerate(out_rows + [mo]):
        grad, aux = meant_for(o * inner + mi)
        for d, peer in enumerate(in_peers):
            place = lax.rem(peer, inner) * outer + o
            await_from(inbox.at[place], rsend.at[0], rrecv.at[place], {"pair": peer})
            grad = grad + inbox[place, pl.ds(0, rows), :]
            aux = aux + inbox[place, pl.ds(rows, AUX), :]
        if z < outer - 1:
            sums[base + z, pl.ds(0, rows), :] = grad
            sums[base + z, pl.ds(rows, AUX), :] = aux
            push(
                sums.at[base + z], inbox.at[arrivals + mo], rsend.at[base + z], rrecv.at[arrivals + mo],
                {"pair": o * inner + mi},
            )
        else:
            total = (grad, aux)

    own_block = (me * rows) // block
    own_offset = pl.multiple_of((me * rows) % block, AUX)
    own_so = gather_start(rows)
    for origin in [me] + out_peers + late_origins():
        own_so = gather_add(own_so, origin, own_block, own_offset, rows)
    own_jones = step_of(own_jones, own_dual, gather_end(own_so, own_jones), own_target)
    vone[mc] = own_jones + own_dual / rho
    chan_spread(vone, 0, rows, 2)
    chan_finish(vone, 0, rows, 2)
    own_target = expand_mine(center_of(vone, 0, rows))
    own_dual = own_dual + rho * (own_jones - own_target)
    grad, aux = total
    for z, o in enumerate(out_rows):
        place = arrivals + o
        await_from(inbox.at[place], rsend.at[0], rrecv.at[place], {"pair": out_peers[z]})
        grad = grad + inbox[place, pl.ds(0, rows), :]
        aux = aux + inbox[place, pl.ds(rows, AUX), :]
    own_jones = step_of(
        own_jones, own_dual, gather_end((grad, aux[0:1], aux[1:2]), own_jones), own_target
    )
    vtwo[mc] = own_jones + own_dual / rho
    chan_spread(vtwo, 0, rows, 3)
    jones_out[...] = own_jones
    chan_finish(vtwo, 0, rows, 3)
    center = center_of(vtwo, 0, rows)
    dual_out[...] = own_dual + rho * (own_jones - expand_mine(center))
    for m in range(poly):
        cons_out[:, m, :] = center[m]
    for copy in pending:
        copy.wait_send()


UNROLL = 4


def basis_table(chan_total):
    middle = np.arange(chan_total, dtype=np.float64) + 0.5
    degree = np.arange(NPOLY, dtype=np.float64)
    normalizer = np.sqrt(np.where(degree == 0, 1.0, 2.0) / chan_total)
    table = np.cos(np.pi * middle[:, None] * degree[None, :] / chan_total) * normalizer[None, :]
    return table.astype(np.float32)


def fused_device(
    jones_init, dual_init, penalty, sky_flux, visibility, phases, pair_ids, counts, slot_flags
):
    rows, chan_dev, width = jones_init.shape
    n, chans = lax.axis_size("pair"), lax.axis_size("chan")
    tiles, slots = visibility.shape[0], visibility.shape[2]
    two = visibility.shape[-1]
    block, dirs = two // 2, penalty.shape[0]
    if tiles != 1 or chan_dev != 1 or width != 128 or rows > block or rows % AUX:
        return per_device(
            jones_init, dual_init, penalty, sky_flux, visibility, phases, pair_ids, counts, slot_flags
        )
    inner = 2 if n % 2 == 0 else 1
    outer = n // inner
    blocks = n * rows // block
    dims = (n, chans, outer, inner, rows, block, slots, dirs, NPOLY, blocks)
    sends = outer - 1 + inner - 1 + (outer - 1) * (inner - 1)
    basis = basis_table(chans)
    part = block + AUX
    f32 = jnp.float32
    vmem = pl.BlockSpec(memory_space=pltpu.VMEM)
    hbm = pl.BlockSpec(memory_space=pltpu.HBM)
    smem = pl.BlockSpec(memory_space=pltpu.SMEM)
    dma = pltpu.SemaphoreType.DMA

    def body(*refs):
        fused_kernel(dims, basis, *refs)

    jones_last, duals_last, center = pl.pallas_call(
        body,
        out_shape=(
            jax.ShapeDtypeStruct((rows, width), f32),
            jax.ShapeDtypeStruct((rows, width), f32),
            jax.ShapeDtypeStruct((rows, NPOLY, width), f32),
        ),
        in_specs=[smem] * 3 + [hbm] * 2 + [vmem] * 2 + [hbm] * 2,
        out_specs=(vmem, vmem, vmem),
        scratch_shapes=[
            pltpu.VMEM((n * rows, width), f32),
            pltpu.VMEM((n * rows, width), f32),
            pltpu.VMEM((chans, rows + two, width), f32),
            pltpu.VMEM((chans, rows, width), f32),
            pltpu.VMEM((chans, rows, width), f32),
            pltpu.VMEM((n, 2 * part, width), f32),
            pltpu.VMEM((two, width), f32),
            pltpu.VMEM((2, slots, 2 * dirs, block), f32),
            pltpu.VMEM((slots, block, width), f32),
            pltpu.VMEM((slots, block, width), f32),
            pltpu.VMEM((slots, block, width), f32),
            pltpu.VMEM((slots, block, width), f32),
            pltpu.VMEM((slots, two, 2 * two), jnp.bfloat16),
            pltpu.VMEM((6, two, width), f32),
            pltpu.VMEM((2 * slots, two, two), jnp.bfloat16),
            pltpu.VMEM((slots, 2, phases.shape[-1]), f32),
            pltpu.VMEM((n, rows + AUX, width), f32),
            pltpu.VMEM((n + outer, rows + AUX, width), f32),
            dma((sends,)), dma((n,)), dma((sends,)), dma((n,)),
            dma((sends,)), dma((n,)), dma((4, chans)), dma((4, chans)),
            dma((n,)), dma((n + outer,)), dma((4,)),
        ],
        compiler_params=pltpu.CompilerParams(
            collective_id=0, has_side_effects=True, vmem_limit_bytes=48 * 1024 * 1024
        ),
    )(
        pair_ids,
        counts,
        slot_flags,
        jones_init.reshape(rows, width),
        dual_init.reshape(rows, width),
        penalty.reshape(1, dirs),
        sky_flux.reshape(sky_flux.shape[1], dirs),
        visibility.reshape(2 * slots, two, two),
        phases.reshape(slots, 2, phases.shape[-1]),
    )
    return (jones_last.reshape(rows, 1, width), duals_last.reshape(rows, 1, width), center)


def solution(mesh):
    in_specs = (
        P("pair", "chan", None),
        P("pair", "chan", None),
        P(),
        P("chan", None, None),
        P("pair", "chan", None, None, None, None),
        P("pair", None, None, None),
        P("pair"),
        P("pair"),
        P("pair", None),
    )
    out_specs = (P("pair", "chan", None), P("pair", "chan", None), P("pair", None, None))
    return jax.shard_map(
        fused_device, mesh=mesh, in_specs=in_specs, out_specs=out_specs, check_vma=False
    )
```

```python
import jax
import jax.numpy as jnp
import numpy as np
from jax import lax
from jax.experimental import pallas as pl
from jax.experimental.pallas import tpu as pltpu
from jax.sharding import PartitionSpec as P

STATIONS = 512
DIRS = 16
BLOCK = 64
TIME = 8
NPOLY = 3
ITERS = 2


STEP_SCALE = 0.3
FULL_PRECISION = lax.Precision.HIGHEST


def pair_tables(block_count):
    row_list = []
    col_list = []
    for row_block in range(block_count):
        for col_block in range(row_block, block_count):
            row_list.append(row_block)
            col_list.append(col_block)
    return (np.array(row_list, np.int32), np.array(col_list, np.int32))


def split_parts(block_jones):
    station_count = block_jones.shape[0]
    chan_count = block_jones.shape[1]
    shaped = block_jones.reshape(station_count, chan_count, 2, 2, 2, DIRS)
    shaped = jnp.transpose(shaped, (2, 1, 0, 3, 5, 4))
    return (shaped[0], shaped[1])


def sky_parts(sky_flux):
    flux_xx = sky_flux[:, 0]
    flux_yy = sky_flux[:, 1]
    cross_re = sky_flux[:, 2]
    cross_im = sky_flux[:, 3]
    zeros_k = jnp.zeros_like(flux_xx)
    real_part = jnp.stack(
        [jnp.stack([flux_xx, cross_re], -1), jnp.stack([cross_re, flux_yy], -1)], -2
    )
    imag_part = jnp.stack(
        [jnp.stack([zeros_k, cross_im], -1), jnp.stack([-cross_im, zeros_k], -1)], -2
    )
    return (real_part, imag_part)


def times_sky(parts, sky_pair):
    jones_re = parts[0][..., None]
    jones_im = parts[1][..., None]
    sky_re = sky_pair[0][:, None, None]
    sky_im = sky_pair[1][:, None, None]
    out_re = jnp.sum(jones_re * sky_re - jones_im * sky_im, axis=-2)
    out_im = jnp.sum(jones_re * sky_im + jones_im * sky_re, axis=-2)
    return (out_re, out_im)


def phase_angles(theta_side, freq_ratio):
    slot_count = theta_side.shape[0]
    shaped = jnp.transpose(theta_side.reshape(slot_count, DIRS, BLOCK), (0, 2, 1))
    angle_all = freq_ratio[:, None, None, None] * shaped[None]
    angle_all = angle_all[:, :, :, None, :, None]
    return (jnp.cos(angle_all), jnp.sin(angle_all))


def rotate_flat(parts, cosines, sines):
    part_re = parts[0][:, None]
    part_im = parts[1][:, None]
    out_re = cosines * part_re - sines * part_im
    out_im = cosines * part_im + sines * part_re
    chan_count = out_re.shape[0]
    slot_count = out_re.shape[1]
    return (
        out_re.reshape(chan_count, slot_count, 2 * BLOCK, 2 * DIRS).astype(jnp.bfloat16),
        out_im.reshape(chan_count, slot_count, 2 * BLOCK, 2 * DIRS).astype(jnp.bfloat16),
    )


def unrotate(product, cosines, sines):
    chan_count = product.shape[0]
    slot_count = product.shape[1]
    shaped = product.reshape(chan_count, slot_count, BLOCK, 2, 2, DIRS, 2)
    neg_re = shaped[:, :, :, :, 0]
    neg_im = shaped[:, :, :, :, 1]
    grad_re = -jnp.sum(neg_re * cosines + neg_im * sines, axis=1)
    grad_im = -jnp.sum(neg_im * cosines - neg_re * sines, axis=1)
    both_parts = jnp.transpose(jnp.stack([grad_re, grad_im], 0), (2, 1, 0, 3, 5, 4))
    return both_parts.reshape(BLOCK, chan_count, 8 * DIRS)


def power_rows(parts):
    power = jnp.sum(parts[0] * parts[0] + parts[1] * parts[1], axis=2)
    power = jnp.transpose(power, (1, 0, 3, 2))
    return power.reshape(power.shape[0], -1)


def slot_terms(vis_part, weights, theta_part, freq_ratio, row_sky, col_sky, col_parts, mask_wide):
    cos_row, sin_row = phase_angles(theta_part[:, 0], freq_ratio)
    cos_col, sin_col = phase_angles(theta_part[:, 1], freq_ratio)
    left_re, left_im = rotate_flat(row_sky, cos_row, sin_row)
    right_re, right_im = rotate_flat(col_sky, cos_col, sin_col)
    conj_re, conj_im = rotate_flat(col_parts, cos_col, sin_col)
    left_side = jnp.concatenate([left_re, left_im], -1)
    model_rhs = jnp.stack(
        [jnp.concatenate([conj_re, conj_im], -1), jnp.concatenate([-conj_im, conj_re], -1)], 2
    )
    predicted = jnp.einsum(
        "ftpk,ftcqk->ftcpq", left_side, model_rhs, preferred_element_type=jnp.float32
    )
    weighting = weights[None, :, None, None, None] * mask_wide
    residual = (weighting * (vis_part.astype(jnp.float32) - predicted)).astype(jnp.bfloat16)
    row_rhs = jnp.stack(
        [jnp.concatenate([right_re, right_im], -1), jnp.concatenate([-right_im, right_re], -1)], 2
    )
    col_rhs = jnp.stack(
        [jnp.concatenate([left_re, left_im], -1), jnp.concatenate([left_im, -left_re], -1)], 2
    )
    row_out = jnp.einsum("ftcpq,ftcqk->ftpk", residual, row_rhs, preferred_element_type=jnp.float32)
    col_out = jnp.einsum("ftcpq,ftcpk->ftqk", residual, col_rhs, preferred_element_type=jnp.float32)
    return (unrotate(row_out, cos_row, sin_row), unrotate(col_out, cos_col, sin_col))


def tile_terms(
    full_jones, sky_pair, freq_ratio, tables, vis_tile, theta_tile, pair_id, kept_slots, flag_row
):
    pair_range = jnp.arange(tables[0].shape[0])
    row_block = jnp.sum(jnp.where(pair_range == pair_id, tables[0], 0)).astype(jnp.int32)
    col_block = jnp.sum(jnp.where(pair_range == pair_id, tables[1], 0)).astype(jnp.int32)
    row_jones = lax.dynamic_slice_in_dim(full_jones, row_block * BLOCK, BLOCK, 0)
    col_jones = lax.dynamic_slice_in_dim(full_jones, col_block * BLOCK, BLOCK, 0)
    row_sky = times_sky(split_parts(row_jones), sky_pair)
    col_parts = split_parts(col_jones)
    col_sky = times_sky(col_parts, sky_pair)
    station_rank = jnp.arange(BLOCK)
    strict = (station_rank[:, None] < station_rank[None, :]) | (row_block != col_block)
    pair_mask = strict.astype(jnp.float32)
    mask_wide = jnp.broadcast_to(pair_mask[:, None, :, None], (BLOCK, 2, BLOCK, 2)).reshape(
        2 * BLOCK, 2 * BLOCK
    )
    weights = flag_row.astype(jnp.float32) * (jnp.arange(TIME) < kept_slots).astype(jnp.float32)
    samples = jnp.sum(weights)
    chan_count = full_jones.shape[1]
    row_grad, col_grad = slot_terms(
        vis_tile, weights, theta_tile, freq_ratio, row_sky, col_sky, col_parts, mask_wide
    )
    row_curv = samples * jnp.dot(pair_mask, power_rows(col_sky), precision=FULL_PRECISION)
    col_curv = samples * jnp.dot(pair_mask.T, power_rows(row_sky), precision=FULL_PRECISION)
    return (
        row_block,
        col_block,
        row_grad,
        col_grad,
        row_curv.reshape(BLOCK, chan_count, 2 * DIRS),
        col_curv.reshape(BLOCK, chan_count, 2 * DIRS),
    )


def add_block(total, start, piece):
    current = lax.dynamic_slice_in_dim(total, start, piece.shape[0], 0)
    return lax.dynamic_update_slice_in_dim(total, current + piece, start, 0)


def data_terms(
    full_jones, sky_pair, freq_ratio, tables, visibility, phases, pair_ids, counts, slot_flags
):
    station_count = full_jones.shape[0]
    chan_count = full_jones.shape[1]
    grad_zero = jnp.zeros((station_count, chan_count, 8 * DIRS), jnp.float32)
    curv_zero = jnp.zeros((station_count, chan_count, 2 * DIRS), jnp.float32)

    def add_tile(carry, tile_inputs):
        grad_sum, curv_sum = carry
        vis_tile, theta_tile, pair_id, kept_slots, flag_row = tile_inputs
        row_block, col_block, row_grad, col_grad, row_curv, col_curv = tile_terms(
            full_jones,
            sky_pair,
            freq_ratio,
            tables,
            vis_tile,
            theta_tile,
            pair_id,
            kept_slots,
            flag_row,
        )
        grad_sum = add_block(grad_sum, row_block * BLOCK, row_grad)
        grad_sum = add_block(grad_sum, col_block * BLOCK, col_grad)
        curv_sum = add_block(curv_sum, row_block * BLOCK, row_curv)
        curv_sum = add_block(curv_sum, col_block * BLOCK, col_curv)
        return ((grad_sum, curv_sum), None)

    totals, unused = lax.scan(
        add_tile, (grad_zero, curv_zero), (visibility, phases, pair_ids, counts, slot_flags)
    )
    return totals


def cosine_basis(chan_total):
    middle = jnp.arange(chan_total, dtype=jnp.float32) + 0.5
    degree = jnp.arange(NPOLY, dtype=jnp.float32)
    normalizer = jnp.sqrt(jnp.where(degree == 0, 1.0, 2.0) / chan_total)
    return jnp.cos(jnp.pi * middle[:, None] * degree[None, :] / chan_total) * normalizer[None, :]


def project(values_all, poly_basis):
    return jnp.sum(poly_basis[None, :, :, None] * values_all[:, :, None, :], axis=1)


def expand(coefficients, poly_basis):
    return jnp.sum(poly_basis[None, :, :, None] * coefficients[:, None, :, :], axis=2)


def jacobi(jones_now, duals_now, gradient, curvature, penalty_full, target):
    divisor = jnp.tile(curvature, (1, 1, 4)) + 0.5 * penalty_full
    return (
        jones_now
        - STEP_SCALE
        * (gradient + 0.5 * penalty_full * (jones_now - target) + 0.5 * duals_now)
        / divisor
    )


def per_device(
    jones_init, dual_init, penalty, sky_flux, visibility, phases, pair_ids, counts, slot_flags
):
    chan_dev = jones_init.shape[1]
    chan_total = chan_dev * lax.axis_size("chan")
    chan_start = lax.axis_index("chan") * chan_dev
    freq_ratio = 1.0 + (chan_start + jnp.arange(chan_dev)).astype(jnp.float32) / chan_total
    poly_basis = lax.dynamic_slice_in_dim(cosine_basis(chan_total), chan_start, chan_dev, 0)
    penalty_full = jnp.tile(penalty, 8)
    sky_pair = sky_parts(sky_flux)
    row_table, col_table = pair_tables(STATIONS // BLOCK)
    tables = (jnp.asarray(row_table), jnp.asarray(col_table))

    def every_consensus(current, dual_now):
        return lax.psum(project(current + dual_now / penalty_full, poly_basis), "chan")

    jones_now, duals_now = (
        lax.all_gather(jones_init, "pair", axis=0, tiled=True),
        lax.all_gather(dual_init, "pair", axis=0, tiled=True),
    )
    center = every_consensus(jones_now, duals_now)
    for outer_round in range(ITERS):
        target = expand(center, poly_basis)
        grad_full, curv_full = data_terms(
            jones_now,
            sky_pair,
            freq_ratio,
            tables,
            visibility,
            phases,
            pair_ids,
            counts,
            slot_flags,
        )
        gradient, curvature = lax.psum((grad_full, curv_full), "pair")
        jones_now = jacobi(jones_now, duals_now, gradient, curvature, penalty_full, target)
        center = every_consensus(jones_now, duals_now)
        duals_now = duals_now + penalty_full * (jones_now - expand(center, poly_basis))
    own_rows = jones_init.shape[0]
    own_start = lax.axis_index("pair") * own_rows
    return (
        lax.dynamic_slice_in_dim(jones_now, own_start, own_rows, 0),
        lax.dynamic_slice_in_dim(duals_now, own_start, own_rows, 0),
        lax.dynamic_slice_in_dim(center, own_start, own_rows, 0),
    )


AUX = 8


def flipped(value, mask):
    bit = 1
    while bit <= mask:
        if mask & bit:
            value = value + bit * (1 - 2 * ((value // bit) % 2))
        bit *= 2
    return value


def fused_kernel(
    dims, basis, pid_ref, cnt_ref, flag_ref, jones_hbm, dual_hbm, rho_ref, sky_ref, vis_hbm, theta_hbm,
    jones_out, dual_out, cons_out,
    jfull, dfull, vzero, vone, vtwo, terms, last, trig, cosr, sinr, cosc, sinc, visp, fac,
    vis_ref, theta_ref, sums, inbox, jsend, jrecv, dsend, drecv, csend, crecv, vsend, vrecv, rsend, rrecv, local,
):
    n, chans, outer, inner, rows, block, slots, dirs, poly, blocks = dims
    width = 8 * dirs
    part = block + AUX
    f32, bf16 = jnp.float32, jnp.bfloat16
    me = lax.axis_index("pair")
    mc = lax.axis_index("chan")
    mo, mi = me // inner, me % inner
    if outer & (outer - 1):
        out_rows = [lax.rem(mo + d, outer) for d in range(1, outer)]
    else:
        out_rows = [flipped(mo, d) for d in range(1, outer)]
    out_peers = [o * inner + mi for o in out_rows]
    in_peers = [mo * inner + lax.rem(mi + d, inner) for d in range(1, inner)]
    chan_peers = [lax.rem(mc + d, chans) for d in range(1, chans)]

    barrier = pltpu.get_barrier_semaphore()
    for peer in out_peers + in_peers:
        pl.semaphore_signal(barrier, inc=1, device_id={"pair": peer}, device_id_type=pl.DeviceIdType.MESH)
    for peer in chan_peers:
        pl.semaphore_signal(barrier, inc=1, device_id={"chan": peer}, device_id_type=pl.DeviceIdType.MESH)
    own_start = pl.multiple_of(me * rows, rows)
    own_jref = jfull.at[pl.ds(own_start, rows)]
    own_dref = dfull.at[pl.ds(own_start, rows)]
    fetches = [
        pltpu.make_async_copy(jones_hbm, own_jref, local.at[0]),
        pltpu.make_async_copy(theta_hbm, theta_ref, local.at[1]),
        pltpu.make_async_copy(dual_hbm, own_dref, local.at[2]),
        pltpu.make_async_copy(vis_hbm, vis_ref, local.at[3]),
    ]
    for fetch in fetches:
        fetch.start()
    pl.semaphore_wait(barrier, len(out_peers) + len(in_peers) + len(chan_peers))

    pending = []

    def push(source, target, ssem, rsem, where):
        copy = pltpu.make_async_remote_copy(
            src_ref=source, dst_ref=target, send_sem=ssem, recv_sem=rsem,
            device_id=where, device_id_type=pl.DeviceIdType.MESH,
        )
        copy.start()
        pending.append(copy)

    def await_from(target, ssem, rsem, where):
        pltpu.make_async_remote_copy(
            src_ref=target, dst_ref=target, send_sem=ssem, recv_sem=rsem,
            device_id=where, device_id_type=pl.DeviceIdType.MESH,
        ).wait_recv()

    def spread(source, slot_of, ssems, rsems):
        for d, peer in enumerate(out_peers):
            push(source, slot_of(me), ssems.at[d], rsems.at[me], {"pair": peer})
        for d, peer in enumerate(in_peers):
            push(source, slot_of(me), ssems.at[outer - 1 + d], rsems.at[me], {"pair": peer})

    def relay_all(streams):
        position = outer - 1 + inner - 1
        for origin in out_peers:
            for slot_of, ssems, rsems in streams:
                await_from(slot_of(origin), ssems.at[0], rsems.at[origin], {"pair": origin})
                for d, peer in enumerate(in_peers):
                    push(
                        slot_of(origin), slot_of(origin), ssems.at[position + d], rsems.at[origin], {"pair": peer}
                    )
            position += inner - 1

    def relay(slot_of, ssems, rsems):
        relay_all([(slot_of, ssems, rsems)])

    def late_origins():
        return [o * inner + lax.rem(peer, inner) for peer in in_peers for o in [mo] + out_rows]

    def await_late(origin, slot_of, ssems, rsems):
        await_from(slot_of(origin), ssems.at[0], rsems.at[origin], {"pair": in_peers[0]})

    def finish(slot_of, ssems, rsems):
        for origin in late_origins():
            await_late(origin, slot_of, ssems, rsems)

    def jslot(origin):
        return jfull.at[pl.ds(pl.multiple_of(origin * rows, rows), rows)]

    def dslot(origin):
        return dfull.at[pl.ds(pl.multiple_of(origin * rows, rows), rows)]

    fetches[0].wait()
    spread(own_jref, jslot, jsend, jrecv)

    def chan_spread(buffer, first, count, level):
        view = buffer.at[mc, pl.ds(first, count)]
        for d, peer in enumerate(chan_peers):
            push(view, view, vsend.at[level, d], vrecv.at[level, mc], {"chan": peer})

    def chan_finish(buffer, first, count, level):
        for peer in chan_peers:
            await_from(
                buffer.at[peer, pl.ds(first, count)], vsend.at[level, 0], vrecv.at[level, peer], {"chan": peer}
            )

    tile_k = lax.broadcasted_iota(jnp.int32, (dirs, width), 1) % dirs
    tiling = (tile_k == lax.broadcasted_iota(jnp.int32, (dirs, width), 0)).astype(f32)

    def widen(values):
        return jnp.dot(values, tiling, precision=FULL_PRECISION, preferred_element_type=f32)

    rho = widen(rho_ref[...])
    sky = widen(sky_ref[...])
    lane = lax.broadcasted_iota(jnp.int32, (1, width), 1)
    imag_lane = (lane // (4 * dirs)) % 2 == 1
    second_i = (lane // (2 * dirs)) % 2 == 1
    second_j = (lane // dirs) % 2 == 1
    sky_same = jnp.where(second_j, sky[1:2], sky[0:1])
    sky_cross = sky[2:3]
    sky_turn = jnp.where(second_j == imag_lane, sky[3:4], -sky[3:4])

    def swap(values, second, gap):
        return jnp.where(second, pltpu.roll(values, gap, 1), pltpu.roll(values, width - gap, 1))

    def swap_c(values):
        return pltpu.roll(values, 4 * dirs, 1)

    def turn(values):
        swapped = swap_c(values)
        return jnp.where(imag_lane, swapped, -swapped)

    def swap_i(values):
        return swap(values, second_i, 2 * dirs)

    def with_sky(values):
        crossed = swap(values, second_j, dirs)
        return values * sky_same + crossed * sky_cross + swap_c(crossed) * sky_turn

    def both_rows(values):
        swapped = swap_i(values)
        return jnp.concatenate(
            [jnp.where(second_i, swapped, values), jnp.where(second_i, values, swapped)], 0
        )

    def power(values):
        squared = values * values
        squared = squared + swap_c(squared)
        return squared + swap_i(squared)

    ratio = 1.0 + mc.astype(f32) / chans
    trig_k = lax.broadcasted_iota(jnp.int32, (6 * dirs, 2 * width), 1)
    trig_row = lax.broadcasted_iota(jnp.int32, (6 * dirs, 2 * width), 0) % (2 * dirs)
    trig_tiling = ((trig_k // width) * dirs + trig_k % dirs == trig_row).astype(f32).astype(bf16)
    fetches[1].wait()
    for side, (cos_ref, sin_ref) in enumerate(((cosr, sinr), (cosc, sinc))):
        angle = theta_ref[:, side, :] * ratio
        cosines, sines = jnp.cos(angle), jnp.sin(angle)
        for k in range(dirs):
            trig[side, :, k, :] = cosines[:, k * block : (k + 1) * block]
            trig[side, :, dirs + k, :] = sines[:, k * block : (k + 1) * block]

        for s in range(slots):
            exact = trig[side, s]
            high = exact.astype(bf16)
            rest = exact - high.astype(f32)
            middle = rest.astype(bf16)
            low = (rest - middle.astype(f32)).astype(bf16)
            wide = lax.dot_general(
                jnp.concatenate([high, middle, low], 0), trig_tiling, (((0,), (0,)), ((), ())),
                preferred_element_type=f32,
            )
            cos_ref[s] = wide[:, :width]
            sin_ref[s] = wide[:, width:]

        if side == 0:
            relay(jslot, jsend, jrecv)

    fetches[2].wait()
    spread(own_dref, dslot, dsend, drecv)
    own_jones = own_jref[...]
    own_dual = own_dref[...]
    vzero[mc, pl.ds(0, rows), :] = own_jones + own_dual / rho
    chan_spread(vzero, 0, rows, 0)
    fetches[3].wait()

    two = 2 * block
    perm_row = lax.broadcasted_iota(jnp.int32, (two, two), 0)
    perm_col = lax.broadcasted_iota(jnp.int32, (two, two), 1)
    unlace = ((perm_row % block) * 2 + perm_row // block == perm_col).astype(f32).astype(bf16)
    lace = ((perm_col % block) * 2 + perm_col // block == perm_row).astype(f32).astype(bf16)

    for s in range(slots):
        for c in range(2):
            half = jnp.dot(unlace, vis_ref[2 * s + c], preferred_element_type=f32).astype(bf16)
            visp[s, :, c * two : (c + 1) * two] = jnp.dot(half, lace, preferred_element_type=f32).astype(bf16)

    pid = pid_ref[0]
    row_block = jnp.int32(0)
    row_first = jnp.int32(0)
    first = 0
    for r in range(1, blocks):
        first += blocks - r + 1
        row_block = jnp.where(pid >= first, r, row_block)
        row_first = jnp.where(pid >= first, first, row_first)
    col_block = row_block + pid - row_first
    apart = jnp.where(row_block == col_block, 0.0, 1.0).astype(f32)
    samples = jnp.float32(0.0)
    for s in range(slots):
        samples = samples + jnp.where(s < cnt_ref[0], flag_ref[0, s], 0).astype(f32)

    def load_block(buffer, which):
        wanted = jnp.full((block, width), which, jnp.int32)
        chosen = jnp.zeros((block, width), f32)
        for b in range(blocks):
            chosen = jnp.where(wanted == b, buffer[b * block : (b + 1) * block, :], chosen)
        return chosen

    upper = (lax.broadcasted_iota(jnp.int32, (two, 2 * two), 0) % block) < (
        lax.broadcasted_iota(jnp.int32, (two, 2 * two), 1) % block
    )
    half_row = lax.broadcasted_iota(jnp.int32, (two, width), 0) // block == 1
    wide_i = (lax.broadcasted_iota(jnp.int32, (two, width), 1) // (2 * dirs)) % 2 == 1
    keep_left = half_row == wide_i
    aux_row = lax.broadcasted_iota(jnp.int32, (AUX, width), 0)

    def data_terms_here(row_jones, col_jones, between=None):
        row_sky, col_sky = with_sky(row_jones), with_sky(col_jones)
        for spot, source in enumerate((row_sky, col_jones, col_sky)):
            fac[2 * spot] = both_rows(source)
            fac[2 * spot + 1] = both_rows(turn(source))
        row_total = samples * jnp.sum(power(row_sky), axis=0, keepdims=True)
        col_total = samples * jnp.sum(power(col_sky), axis=0, keepdims=True)
        row_id = row_block.astype(f32)
        col_id = col_block.astype(f32)
        same = samples * (1.0 - apart)
        aux_r = jnp.where(aux_row == 0, col_total, jnp.where(aux_row == 1, same, row_id))
        aux_c = jnp.where(aux_row == 0, row_total * apart, jnp.where(aux_row == 1, 0.0, col_id))

        def slot_step(s, carry):
            row_sum, col_sum = carry
            weight = jnp.where(s < cnt_ref[0], flag_ref[0, s], 0).astype(f32)
            weighting = jnp.where(upper, weight, weight * apart)
            cos_r, sin_r = cosr[s], sinr[s]
            cos_c, sin_c = cosc[s], sinc[s]
            wide = [jnp.concatenate([x, x], 0) for x in (cos_r, sin_r, cos_c, sin_c)]

            def rotated(spot, cosines, sines):
                plain, turned = fac[2 * spot], fac[2 * spot + 1]
                return (
                    cosines * plain + sines * turned,
                    cosines * turned - sines * plain,
                )

            left, left_turn = rotated(0, wide[0], wide[1])
            conj, conj_turn = rotated(1, wide[2], wide[3])
            right, right_turn = rotated(2, wide[2], wide[3])
            left_only = jnp.where(keep_left, left, 0.0).astype(bf16)
            model_rhs = jnp.concatenate([conj.astype(bf16), conj_turn.astype(bf16)], 0)
            predicted = lax.dot_general(
                left_only, model_rhs, (((1,), (1,)), ((), ())), preferred_element_type=f32
            )
            residual = (weighting * (visp[s].astype(f32) - predicted)).astype(bf16)
            row_rhs = jnp.concatenate([right.astype(bf16), right_turn.astype(bf16)], 0)
            row_out = jnp.dot(residual, row_rhs, preferred_element_type=f32)
            col_out = lax.dot_general(
                residual[:, :two], left.astype(bf16), (((0,), (0,)), ((), ())), preferred_element_type=f32
            ) - lax.dot_general(
                residual[:, two:], left_turn.astype(bf16), (((0,), (0,)), ((), ())), preferred_element_type=f32
            )
            row_pick = jnp.where(second_i, row_out[block:], row_out[:block])
            col_pick = jnp.where(second_i, col_out[block:], col_out[:block])
            row_sum = row_sum + (sin_r * turn(row_pick) - cos_r * row_pick)
            col_sum = col_sum + (sin_c * turn(col_pick) - cos_c * col_pick)
            return (row_sum, col_sum)

        zero = jnp.zeros((block, width), f32)
        middle = slots // 2 if between else slots
        sums_here = lax.fori_loop(0, middle, slot_step, (zero, zero), unroll=UNROLL)
        if between:
            between()
            sums_here = lax.fori_loop(middle, slots, slot_step, sums_here, unroll=UNROLL)
        row_grad, col_grad = sums_here
        return row_grad, aux_r, col_grad, aux_c

    def term_half(side):
        return lambda origin: terms.at[origin, pl.ds(side * part, part)]

    term_streams = [(term_half(side), csend.at[side], crecv.at[side]) for side in range(2)]

    def gather_start(count):
        return (
            jnp.zeros((count, width), f32), jnp.zeros((1, width), f32), jnp.zeros((1, width), f32)
        )

    def gather_add(so_far, origin, block_id, offset, count):
        wanted = block_id.astype(f32)
        grad, shared, alone = so_far
        for side in range(2):
            base = side * part
            aux = terms[origin, pl.ds(base + block, AUX), :]
            hit = aux[2:3] == wanted
            grad = grad + jnp.where(hit, terms[origin, pl.ds(base + offset, count), :], 0.0)
            shared = shared + jnp.where(hit, aux[0:1], 0.0)
            alone = alone + jnp.where(hit, aux[1:2], 0.0)
        return grad, shared, alone

    def gather_end(so_far, jones_here):
        grad, shared, alone = so_far
        return grad, shared - alone * power(with_sky(jones_here))

    def center_of(buffer, first, count):
        values = [buffer[f, pl.ds(first, count), :] for f in range(chans)]
        return [sum(float(basis[f, m]) * values[f] for f in range(chans)) for m in range(poly)]

    mine = []
    for m in range(poly):
        coefficient = jnp.float32(basis[0, m])
        for f in range(1, chans):
            coefficient = jnp.where(mc == f, jnp.float32(basis[f, m]), coefficient)
        mine.append(coefficient)

    def expand_mine(center):
        return sum(mine[m] * center[m] for m in range(poly))

    def step_of(jones_here, duals_here, terms_here, target):
        gradient, curvature = terms_here
        return jones_here - STEP_SCALE * (
            gradient + 0.5 * rho * (jones_here - target) + 0.5 * duals_here
        ) / (curvature + 0.5 * rho)

    finish(jslot, jsend, jrecv)
    row_jones = load_block(jfull, row_block)
    col_jones = load_block(jfull, col_block)
    row_grad, aux_r, col_grad, aux_c = data_terms_here(
        row_jones, col_jones, lambda: relay(dslot, dsend, drecv)
    )
    terms[me, pl.ds(0, block), :] = row_grad
    terms[me, pl.ds(block, AUX), :] = aux_r
    terms[me, pl.ds(part, block), :] = col_grad
    terms[me, pl.ds(part + block, AUX), :] = aux_c
    for slot_of, ssems, rsems in term_streams:
        spread(slot_of(me), slot_of, ssems, rsems)
    finish(dslot, dsend, drecv)
    row_dual = load_block(dfull, row_block)
    col_dual = load_block(dfull, col_block)
    vzero[mc, pl.ds(rows, block), :] = row_jones + row_dual / rho
    vzero[mc, pl.ds(rows + block, block), :] = col_jones + col_dual / rho
    chan_spread(vzero, rows, two, 1)
    relay_all(term_streams)
    row_so = gather_start(block)
    col_so = gather_start(block)
    for origin in [me] + out_peers:
        row_so = gather_add(row_so, origin, row_block, 0, block)
        col_so = gather_add(col_so, origin, col_block, 0, block)
    chan_finish(vzero, 0, rows, 0)
    chan_finish(vzero, rows, two, 1)
    own_target = expand_mine(center_of(vzero, 0, rows))
    row_target = expand_mine(center_of(vzero, rows, block))
    col_target = expand_mine(center_of(vzero, rows + block, block))
    for origin in late_origins():
        for stream in term_streams:
            await_late(origin, *stream)
        row_so = gather_add(row_so, origin, row_block, 0, block)
        col_so = gather_add(col_so, origin, col_block, 0, block)
    row_next = step_of(row_jones, row_dual, gather_end(row_so, row_jones), row_target)
    col_next = step_of(col_jones, col_dual, gather_end(col_so, col_jones), col_target)

    row_grad, aux_r, col_grad, aux_c = data_terms_here(row_next, col_next)
    last[pl.ds(0, block), :] = row_grad
    last[pl.ds(block, block), :] = col_grad
    message = rows + AUX

    def meant_for(owner):
        owner_block = (owner * rows) // block
        offset = pl.multiple_of((owner * rows) % block, AUX)
        to_row = jnp.where(jnp.full((1, width), row_block, jnp.int32) == owner_block, 1, 0) == 1
        to_col = jnp.where(jnp.full((1, width), col_block, jnp.int32) == owner_block, 1, 0) == 1
        grad = jnp.where(to_row, last[pl.ds(offset, rows), :], 0.0) + jnp.where(
            to_col, last[pl.ds(block + offset, rows), :], 0.0
        )
        return grad, jnp.where(to_row, aux_r, 0.0) + jnp.where(to_col, aux_c, 0.0)

    for d, peer in enumerate(in_peers):
        far = lax.rem(peer, inner)
        for z, o in enumerate(out_rows + [mo]):
            spot = d * outer + z
            grad, aux = meant_for(o * inner + far)
            sums[spot, pl.ds(0, rows), :] = grad
            sums[spot, pl.ds(rows, AUX), :] = aux
            push(
                sums.at[spot], inbox.at[mi * outer + o], rsend.at[spot], rrecv.at[mi * outer + o], {"pair": peer}
            )
    base = (inner - 1) * outer
    arrivals = inner * outer
    total = None
    for z, o in enumerate(out_rows + [mo]):
        grad, aux = meant_for(o * inner + mi)
        for d, peer in enumerate(in_peers):
            place = lax.rem(peer, inner) * outer + o
            await_from(inbox.at[place], rsend.at[0], rrecv.at[place], {"pair": peer})
            grad = grad + inbox[place, pl.ds(0, rows), :]
            aux = aux + inbox[place, pl.ds(rows, AUX), :]
        if z < outer - 1:
            sums[base + z, pl.ds(0, rows), :] = grad
            sums[base + z, pl.ds(rows, AUX), :] = aux
            push(
                sums.at[base + z], inbox.at[arrivals + mo], rsend.at[base + z], rrecv.at[arrivals + mo],
                {"pair": o * inner + mi},
            )
        else:
            total = (grad, aux)

    own_block = (me * rows) // block
    own_offset = pl.multiple_of((me * rows) % block, AUX)
    own_so = gather_start(rows)
    for origin in [me] + out_peers + late_origins():
        own_so = gather_add(own_so, origin, own_block, own_offset, rows)
    own_jones = step_of(own_jones, own_dual, gather_end(own_so, own_jones), own_target)
    vone[mc] = own_jones + own_dual / rho
    chan_spread(vone, 0, rows, 2)
    chan_finish(vone, 0, rows, 2)
    own_target = expand_mine(center_of(vone, 0, rows))
    own_dual = own_dual + rho * (own_jones - own_target)
    grad, aux = total
    for z, o in enumerate(out_rows):
        place = arrivals + o
        await_from(inbox.at[place], rsend.at[0], rrecv.at[place], {"pair": out_peers[z]})
        grad = grad + inbox[place, pl.ds(0, rows), :]
        aux = aux + inbox[place, pl.ds(rows, AUX), :]
    own_jones = step_of(
        own_jones, own_dual, gather_end((grad, aux[0:1], aux[1:2]), own_jones), own_target
    )
    vtwo[mc] = own_jones + own_dual / rho
    chan_spread(vtwo, 0, rows, 3)
    jones_out[...] = own_jones
    chan_finish(vtwo, 0, rows, 3)
    center = center_of(vtwo, 0, rows)
    dual_out[...] = own_dual + rho * (own_jones - expand_mine(center))
    for m in range(poly):
        cons_out[:, m, :] = center[m]
    for copy in pending:
        copy.wait_send()


UNROLL = 4


def basis_table(chan_total):
    middle = np.arange(chan_total, dtype=np.float64) + 0.5
    degree = np.arange(NPOLY, dtype=np.float64)
    normalizer = np.sqrt(np.where(degree == 0, 1.0, 2.0) / chan_total)
    table = np.cos(np.pi * middle[:, None] * degree[None, :] / chan_total) * normalizer[None, :]
    return table.astype(np.float32)


def fused_device(
    jones_init, dual_init, penalty, sky_flux, visibility, phases, pair_ids, counts, slot_flags
):
    rows, chan_dev, width = jones_init.shape
    n, chans = lax.axis_size("pair"), lax.axis_size("chan")
    tiles, slots = visibility.shape[0], visibility.shape[2]
    two = visibility.shape[-1]
    block, dirs = two // 2, penalty.shape[0]
    if tiles != 1 or chan_dev != 1 or width != 128 or rows > block or rows % AUX:
        return per_device(
            jones_init, dual_init, penalty, sky_flux, visibility, phases, pair_ids, counts, slot_flags
        )
    inner = 2 if n % 2 == 0 else 1
    outer = n // inner
    blocks = n * rows // block
    dims = (n, chans, outer, inner, rows, block, slots, dirs, NPOLY, blocks)
    sends = outer - 1 + inner - 1 + (outer - 1) * (inner - 1)
    basis = basis_table(chans)
    part = block + AUX
    f32 = jnp.float32
    vmem = pl.BlockSpec(memory_space=pltpu.VMEM)
    hbm = pl.BlockSpec(memory_space=pltpu.HBM)
    smem = pl.BlockSpec(memory_space=pltpu.SMEM)
    dma = pltpu.SemaphoreType.DMA

    def body(*refs):
        fused_kernel(dims, basis, *refs)

    jones_last, duals_last, center = pl.pallas_call(
        body,
        out_shape=(
            jax.ShapeDtypeStruct((rows, width), f32),
            jax.ShapeDtypeStruct((rows, width), f32),
            jax.ShapeDtypeStruct((rows, NPOLY, width), f32),
        ),
        in_specs=[smem] * 3 + [hbm] * 2 + [vmem] * 2 + [hbm] * 2,
        out_specs=(vmem, vmem, vmem),
        scratch_shapes=[
            pltpu.VMEM((n * rows, width), f32),
            pltpu.VMEM((n * rows, width), f32),
            pltpu.VMEM((chans, rows + two, width), f32),
            pltpu.VMEM((chans, rows, width), f32),
            pltpu.VMEM((chans, rows, width), f32),
            pltpu.VMEM((n, 2 * part, width), f32),
            pltpu.VMEM((two, width), f32),
            pltpu.VMEM((2, slots, 2 * dirs, block), f32),
            pltpu.VMEM((slots, block, width), f32),
            pltpu.VMEM((slots, block, width), f32),
            pltpu.VMEM((slots, block, width), f32),
            pltpu.VMEM((slots, block, width), f32),
            pltpu.VMEM((slots, two, 2 * two), jnp.bfloat16),
            pltpu.VMEM((6, two, width), f32),
            pltpu.VMEM((2 * slots, two, two), jnp.bfloat16),
            pltpu.VMEM((slots, 2, phases.shape[-1]), f32),
            pltpu.VMEM((n, rows + AUX, width), f32),
            pltpu.VMEM((n + outer, rows + AUX, width), f32),
            dma((sends,)), dma((n,)), dma((sends,)), dma((n,)),
            dma((2, sends)), dma((2, n)), dma((4, chans)), dma((4, chans)),
            dma((n,)), dma((n + outer,)), dma((4,)),
        ],
        compiler_params=pltpu.CompilerParams(
            collective_id=0, has_side_effects=True, vmem_limit_bytes=67043328
        ),
    )(
        pair_ids,
        counts,
        slot_flags,
        jones_init.reshape(rows, width),
        dual_init.reshape(rows, width),
        penalty.reshape(1, dirs),
        sky_flux.reshape(sky_flux.shape[1], dirs),
        visibility.reshape(2 * slots, two, two),
        phases.reshape(slots, 2, phases.shape[-1]),
    )
    return (jones_last.reshape(rows, 1, width), duals_last.reshape(rows, 1, width), center)


def solution(mesh):
    in_specs = (
        P("pair", "chan", None),
        P("pair", "chan", None),
        P(),
        P("chan", None, None),
        P("pair", "chan", None, None, None, None),
        P("pair", None, None, None),
        P("pair"),
        P("pair"),
        P("pair", None),
    )
    out_specs = (P("pair", "chan", None), P("pair", "chan", None), P("pair", None, None))
    return jax.shard_map(
        fused_device, mesh=mesh, in_specs=in_specs, out_specs=out_specs, check_vma=False
    )
```
